128 devices in a mesh: pair: 8 (over y_hi, x), slab: 16 (over y_lo, z, core).
Axes of the slice: x: 4, y: 4 (y_hi: 2, y_lo: 2; y = y_hi * 2 + y_lo), z: 4, core: 2. Of those that a mesh axis runs over, the one named last changes fastest.
Arguments:
- pair_density: bfloat16 [24576, 49152], P('pair', 'slab'), may hold values from -6 to 6
- subspace: bfloat16 [49152, 512], P('slab'), may hold values from -0.02734375 to 0.02734375
- band_valence: int32 [24576], P('pair'), may hold values from 0 to 510, as said below
- band_conduction: int32 [24576], P('pair'), may hold values from 1 to 511, as said below
- occupied: int32 [512], replicated, may hold values from 0 to 1, as said below
- energies: float32 [512], replicated, may hold values from -1 to 1
Outputs:
- chi_panel: float32 [512, 49152], P('pair', 'slab')
- subspace_chi: float32 [512, 512], P('slab', 'pair')
The draws below stay inside these ranges and needn't reach their ends.
Inputs may be any that keep to these rules, and one draw needn't show every extreme that they name: Exactly half of the 512 bands are occupied. `band_valence`: every entry names a band that occupied marks as occupied. `band_conduction`: every entry names a band that occupied marks as unoccupied.
All inputs are finite; a program needn't handle non-finite values.
Results may differ from the reference program's by a relative error of at most 0.0024.
Values sent between devices are 32-bit elements; how exact they have to be, the bound alone decides.
A program may use at most 128 MiB of HBM per device.

```python
import math
import jax
import jax.numpy as jnp
from jax import lax

G = 49152
NB = 512
NBANDS = 512
PAIRS = 24576


def band_sets(key):
    half = NBANDS // 2
    shuffled = jax.random.permutation(jax.random.fold_in(key, 17), NBANDS - 4).astype(jnp.int32) + 2
    filled_list = jnp.concatenate([jnp.array([0, NBANDS - 2], dtype=jnp.int32), shuffled[:half - 2]])
    empty_list = jnp.concatenate([jnp.array([NBANDS - 1, 1], dtype=jnp.int32), shuffled[half - 2:]])
    occupied = jnp.zeros((NBANDS,), jnp.int32).at[filled_list].set(1)
    low_pick = jax.random.randint(jax.random.fold_in(key, 29), (PAIRS,), 0, half)
    high_pick = jax.random.randint(jax.random.fold_in(key, 41), (PAIRS,), 0, half)
    valence = filled_list[low_pick].at[0].set(0).at[1].set(NBANDS - 2)
    conduction = empty_list[high_pick].at[0].set(NBANDS - 1).at[1].set(1)
    return (valence.astype(jnp.int32), conduction.astype(jnp.int32), occupied)


def draw_band_valence(key, part):
    return band_sets(key)[0]


def draw_band_conduction(key, part):
    return band_sets(key)[1]


def draw_occupied(key, part):
    return band_sets(key)[2]


def block_levels(own_key, extent, shards, smallest, top_value):
    factor_of = 1.0
    for axis_at, shards_of in shards:
        draws = jax.random.uniform(jax.random.fold_in(jax.random.fold_in(own_key, 6), axis_at), (shards_of,), jnp.float32, smallest / len(shards), top_value / len(shards))
        factor_of = factor_of * jnp.repeat(jnp.exp(draws), extent[axis_at] // shards_of).reshape((-1,) + (1,) * (len(extent) - 1 - axis_at))
    return factor_of


def gaussian(key, dims, deviation, bound, pieces=(), held_as=jnp.bfloat16):
    level = block_levels(key, dims, pieces, -0.22, 0.18) if pieces else 1.0
    values = jax.random.normal(key, dims, jnp.float32) * deviation * level
    return jnp.minimum(jnp.maximum(values, -bound), bound).astype(held_as)


def setup_inputs(seed: int = 0) -> dict:
    key_list = jax.random.split(jax.random.key(seed), 7)
    pair_density = gaussian(key_list[0], (PAIRS, G), 1.0, 6.0, ((0, 8), (1, 16)))
    subspace = gaussian(key_list[1], (G, NB), G ** -0.5, 0.02734375, ((0, 16),))
    band_valence = draw_band_valence(jax.random.fold_in(key_list[6], 71), 0)
    band_conduction = draw_band_conduction(jax.random.fold_in(key_list[6], 71), 0)
    occupied = draw_occupied(jax.random.fold_in(key_list[6], 71), 0)
    energies = jnp.clip(jax.random.uniform(key_list[5], (NBANDS,), jnp.float32, -1.0, 1.0), -1.0, 1.0)
    return {"pair_density": pair_density, "subspace": subspace, "band_valence": band_valence, "band_conduction": band_conduction, "occupied": occupied, "energies": energies}


def pair_weights(band_valence, band_conduction, occupied, energies):
    energy_low = energies[band_valence]
    energy_high = energies[band_conduction]
    filled_low = occupied[band_valence].astype(jnp.float32)
    filled_high = occupied[band_conduction].astype(jnp.float32)
    scale = 1.0 / math.sqrt(PAIRS)
    return -2.0 * filled_low * (1.0 - filled_high) / (jnp.abs(energy_high - energy_low) + 0.5) * scale

def reference(pair_density, subspace, band_valence, band_conduction, occupied, energies):
    coefficient = jnp.dot(pair_density, subspace, preferred_element_type=jnp.float32)
    pair_weight = pair_weights(band_valence, band_conduction, occupied, energies)
    weighted = (coefficient * pair_weight[:, None]).astype(jnp.bfloat16)
    chi_panel = lax.dot_general(weighted, pair_density, (((0,), (0,)), ((), ())), preferred_element_type=jnp.float32)
    subspace_chi = lax.dot_general(subspace.astype(jnp.float32), chi_panel, (((0,), (1,)), ((), ())), precision=lax.Precision.HIGHEST)
    return (chi_panel, subspace_chi)
```

```python
import functools
import math

import jax
import jax.numpy as jnp
from jax import lax
from jax.experimental import pallas as pl
from jax.experimental.pallas import tpu as pltpu
from jax.sharding import PartitionSpec as P

MESH = pl.DeviceIdType.MESH
F32, BF16 = jnp.float32, jnp.bfloat16

CHUNKS = 4
PARTS = 2
SUM_MODE = "BBBB"
PANEL_MODE = "BBBB"
ORDER = (
    ("A",), ("B", 0), ("B", 1), ("R1", 0), ("R1", 1), ("B", 2), ("B", 3), ("R2", 0),
    ("R1", 2), ("R1", 3), ("R2", 1), ("R3", 0), ("R2", 2), ("R2", 3), ("R3", 1), ("R4", 0),
    ("R3", 2), ("R3", 3), ("R4", 1), ("G2", 0), ("R4", 2), ("R4", 3), ("G2", 1), ("G3", 0),
    ("G4", 0), ("G2", 2), ("W", 0), ("G2", 3), ("F1", 0, 0), ("G3", 1), ("F1", 0, 1), ("G3", 2),
    ("G4", 1), ("G3", 3), ("F2", 0, 0), ("W", 1), ("G4", 2), ("F2", 0, 1), ("F1", 1, 0), ("G4", 3),
    ("F3", 0, 0), ("F3", 0, 1), ("F1", 1, 1), ("W", 2), ("F1", 2, 0), ("F4", 0, 0), ("F2", 1, 0), ("F1", 2, 1),
    ("F4", 0, 1), ("W", 3), ("F2", 1, 1), ("F1", 3, 0), ("F3", 1, 0), ("F2", 2, 0), ("F1", 3, 1), ("F2", 2, 1),
    ("F3", 1, 1), ("S1",), ("F2", 3, 0), ("F4", 1, 0), ("F3", 2, 0), ("F2", 3, 1), ("F3", 2, 1), ("F4", 1, 1),
    ("S2",), ("F3", 3, 0), ("F4", 2, 0), ("F3", 3, 1), ("F4", 2, 1), ("F4", 3, 0), ("F4", 3, 1),
)


def lookup(indices, table):
    levels = jnp.arange(table.shape[0], dtype=jnp.int32)
    one_hot = (indices[:, None] == levels[None, :]).astype(F32)
    return jnp.dot(one_hot, table, precision=lax.Precision.HIGHEST)


class Links:
    def __init__(self, send_sem, recv_sem):
        self.send_sem, self.recv_sem = send_sem, recv_sem
        self.made = {}

    def send(self, name, source, target, device):
        at = len(self.made)
        copy = pltpu.make_async_remote_copy(
            source, target, self.send_sem.at[at], self.recv_sem.at[at], device_id=device, device_id_type=MESH
        )
        copy.start()
        self.made[name] = copy

    def wait(self, *names):
        for name in names:
            self.made[name].wait_recv()

    def finish(self):
        for copy in self.made.values():
            copy.wait_send()


def ring_sum(links, tag, mode, piece, slots, ring_up, ring_down, across, half):
    lo, hi = pl.ds(0, half), pl.ds(half, half)

    def add(ref, *others):
        total = ref[...]
        for other in others:
            total = total + other[...]
        ref[...] = total

    def first():
        if mode == "B":
            links.send((tag, "y1"), piece(2, 1), slots.at[6], across)
            links.send((tag, "p1"), piece(1, 1), slots.at[0], ring_up)
            links.send((tag, "m1"), piece(3, 1), slots.at[1], ring_down)
        else:
            links.send((tag, "p2"), piece(2, 0), slots.at[2], ring_up)
            links.send((tag, "m2"), piece(2, 1), slots.at[3], ring_down)
            links.send((tag, "p1"), piece(1, 1), slots.at[0], ring_up)
            links.send((tag, "m1"), piece(3, 0), slots.at[1], ring_down)

    def second():
        if mode == "B":
            links.wait((tag, "y1"))
            add(piece(2, 0), slots.at[6])
            links.send((tag, "p2"), piece(2, 0).at[lo], slots.at[2, lo], ring_up)
            links.send((tag, "m2"), piece(2, 0).at[hi], slots.at[3, hi], ring_down)
        else:
            links.wait((tag, "p2"))
            add(piece(1, 0), slots.at[2])
            links.send((tag, "p3"), piece(1, 0), slots.at[4], ring_up)
            links.wait((tag, "m2"))
            add(piece(3, 1), slots.at[3])
            links.send((tag, "m3"), piece(3, 1), slots.at[5], ring_down)

    def third():
        if mode == "B":
            links.wait((tag, "p1"), (tag, "m1"))
            add(piece(0, 1), slots.at[0], slots.at[1])
            links.send((tag, "y3"), piece(0, 1), slots.at[7], across)
            links.wait((tag, "p2"))
            add(piece(1, 0).at[lo], slots.at[2, lo])
            links.send((tag, "p3"), piece(1, 0), slots.at[4], ring_up)
            links.wait((tag, "m2"))
            add(piece(3, 0).at[hi], slots.at[3, hi])
            links.send((tag, "m3"), piece(3, 0), slots.at[5], ring_down)
        else:
            links.wait((tag, "p1"), (tag, "m3"))
            add(piece(0, 1), slots.at[0], slots.at[5])
            links.send((tag, "y3"), piece(0, 1), slots.at[7], across)

    def last():
        if mode == "B":
            links.wait((tag, "y3"), (tag, "p3"), (tag, "m3"))
            return piece(0, 0)[...] + slots[4] + slots[5] + slots[7]
        links.wait((tag, "m1"), (tag, "p3"), (tag, "y3"))
        return piece(0, 0)[...] + slots[1] + slots[4] + slots[7]

    return first, second, third, last


def kernel(
    a_hbm, s_hbm, w_ref, chi_out, sub_out,
    a_v, s_v, sp, coeff, core_in, sum_in, full, wt, chi, panel_in, sub_mine, sub_in,
    load_sem, core_send, core_recv, send_sem, recv_sem,
):
    pairs, depth = a_v.shape
    nb = s_v.shape[1]
    width = nb // CHUNKS
    block = pairs // 8
    own = block // 2
    rows_q = width // 8
    cols = depth // PARTS

    pair, slab = lax.axis_index("pair"), lax.axis_index("slab")
    y_hi, x = lax.div(pair, 4), lax.rem(pair, 4)
    y_lo, z, core = lax.div(slab, 8), lax.rem(lax.div(slab, 2), 4), lax.rem(slab, 2)

    def slab_of(y, zz, c):
        return (pair, y * 8 + zz * 2 + c)

    def pair_of(y, xx):
        return (y * 4 + xx, slab)

    def up(v, d):
        return lax.rem(v + d, 4)

    z_up, z_down = slab_of(y_lo, up(z, 1), core), slab_of(y_lo, up(z, 3), core)
    y_across, other_core = slab_of(1 - y_lo, z, core), slab_of(y_lo, z, 1 - core)
    x_up, x_down, hi_across = pair_of(y_hi, up(x, 1)), pair_of(y_hi, up(x, 3)), pair_of(1 - y_hi, x)

    def peer(d):
        return (lax.rem(pair + d, 8), slab)

    Z_ORDER = (2, 1, 3, 0)

    def nth_z(j):
        step = jnp.where(j == 0, 2, jnp.where(j == 1, 1, jnp.where(j == 2, 3, 0)))
        return lax.rem(z + step, 4)

    def nth_rows(i):
        other = jnp.where(i < 4, 1 - core, core)
        j = lax.rem(i, 4)
        return pl.ds(pl.multiple_of((other * 4 + nth_z(j)) * block, block), block)

    def a_load(i):
        return pltpu.make_async_copy(a_hbm.at[nth_rows(i)], a_v.at[nth_rows(i)], load_sem.at[i])

    s_load = pltpu.make_async_copy(s_hbm, s_v, load_sem.at[8])
    s_load.start()
    for i in range(8):
        a_load(i).start()

    barrier = pltpu.get_barrier_semaphore()
    greeted = [z_up, z_down, y_across, other_core] + [peer(d) for d in range(1, 8)]
    for device in greeted:
        pl.semaphore_signal(barrier, inc=1, device_id=device, device_id_type=MESH)

    links = Links(send_sem, recv_sem)

    def choose(kp):
        to = lax.broadcasted_iota(jnp.int32, (nb, 2 * width), 1)
        frm = lax.broadcasted_iota(jnp.int32, (nb, 2 * width), 0)
        k = kp * 2 + to // width
        b = (lax.rem(to, width) // rows_q) * (nb // 8) + k * rows_q + lax.rem(to, rows_q)
        pick = jnp.where(frm == b, 1.0, 0.0).astype(BF16)

        @pl.loop(0, 8)
        def _(i):
            rows = pl.ds(pl.multiple_of(i * block, block), block)
            sp[rows, :] = jnp.dot(s_v[rows, :], pick, preferred_element_type=F32).astype(BF16)

    def core_copy(k, j):
        there = pl.ds(pl.multiple_of(nth_z(j) * block, block), block)
        return pltpu.make_async_remote_copy(
            coeff.at[k, nth_rows(j)], core_in.at[k, there], core_send.at[k, j], core_recv.at[k, j],
            device_id=other_core, device_id_type=MESH,
        )

    def product(kp, start, stop):
        @pl.loop(start, stop)
        def _(i):
            rows = nth_rows(i)
            if kp == 0:
                a_load(i).wait()
            part = jnp.dot(a_v[rows, :], sp[...], preferred_element_type=F32)
            for h in range(2):
                coeff[2 * kp + h, rows, :] = part[:, h * width : (h + 1) * width]

            @pl.when(i < 4)
            def _():
                for h in range(2):
                    core_copy(2 * kp + h, i).start()

    def owner_rows(z_at, y_at):
        return pl.ds(pl.multiple_of((core * 4 + z_at) * block + y_at * own, own), own)

    steps = {}
    for k in range(CHUNKS):
        get = lambda dr, da, k=k: coeff.at[k, owner_rows(up(z, dr), (1 - y_lo) if da else y_lo)]
        first, second, third, last = ring_sum(
            links, ("R", k), SUM_MODE[k], get, sum_in.at[k], z_up, z_down, y_across, own // 2
        )

        def r1(k=k, first=first):
            for j in range(4):
                core_copy(k, j).wait_recv()
                here = pl.ds(pl.multiple_of((core * 4 + nth_z(j)) * block, block), block)
                there = pl.ds(pl.multiple_of(nth_z(j) * block, block), block)
                coeff[k, here, :] = coeff[k, here, :] + core_in[k, there, :]
            first()

        def spread(name, z_at, y_at, device, k=k, part=None):
            rows = owner_rows(z_at, y_at)
            if part is not None:
                start = (core * 4 + z_at) * block + y_at * own + part * (own // 2)
                rows = pl.ds(pl.multiple_of(start, own // 2), own // 2)
            links.send((name, k), full.at[k, rows], full.at[k, rows], device)

        def r4(k=k, last=last, spread=spread):
            full[k, owner_rows(z, y_lo), :] = last()
            spread("y1", z, y_lo, y_across)
            spread("p1", z, y_lo, z_up)
            spread("m1", z, y_lo, z_down)
            spread("c0", z, y_lo, other_core)

        def g2(k=k, spread=spread):
            links.wait(("p1", k))
            spread("p2", up(z, 3), y_lo, z_up, part=0)
            links.wait(("m1", k))
            spread("m2", up(z, 1), y_lo, z_down, part=1)
            links.wait(("y1", k))
            spread("p3", z, 1 - y_lo, z_up)
            spread("m3", z, 1 - y_lo, z_down)
            spread("c1", up(z, 3), y_lo, other_core)
            spread("c2", up(z, 1), y_lo, other_core)
            spread("c3", z, 1 - y_lo, other_core)

        def g3(k=k, spread=spread):
            links.wait(("p2", k), ("m2", k))
            spread("y3", up(z, 2), y_lo, y_across)
            spread("c4", up(z, 2), y_lo, other_core)

        def g4(k=k, spread=spread):
            links.wait(("p3", k), ("m3", k))
            spread("c5", up(z, 3), 1 - y_lo, other_core)
            spread("c6", up(z, 1), 1 - y_lo, other_core)
            links.wait(("y3", k))
            spread("c7", up(z, 2), 1 - y_lo, other_core)

        def weigh(k=k):
            links.wait(*[(f"c{i}", k) for i in range(8)])

            @pl.loop(0, 8)
            def _(i):
                at = pl.ds(pl.multiple_of(i * block, block), block)
                wt[k, :, at] = (full[k, at, :].T * w_ref[:, at]).astype(BF16)

        steps["R1", k], steps["R2", k], steps["R3", k], steps["R4", k] = r1, second, third, r4
        steps["G2", k], steps["G3", k], steps["G4", k], steps["W", k] = g2, g3, g4, weigh

        for g in range(PARTS):
            def rows_of(dx, dy, k=k, g=g):
                q = ((1 - y_hi) if dy else y_hi) * 4 + up(x, dx)
                return chi.at[k, g, pl.ds(pl.multiple_of(q * rows_q, rows_q), rows_q)]

            first, second, third, last = ring_sum(
                links, ("F", k, g), PANEL_MODE[k], rows_of, panel_in.at[k, g], x_up, x_down, hi_across, rows_q // 2
            )

            def f1(k=k, g=g, first=first):
                tile = cols // 3

                @pl.loop(0, 3)
                def _(i):
                    src = pl.ds(pl.multiple_of(g * cols + i * tile, tile), tile)
                    dst = pl.ds(pl.multiple_of(i * tile, tile), tile)
                    chi[k, g, :, dst] = jnp.dot(wt[k], a_v[:, src], preferred_element_type=F32)

                first()

            def f4(k=k, g=g, last=last):
                chi_out[k * rows_q : (k + 1) * rows_q, g * cols : (g + 1) * cols] = last()

            steps["F1", k, g], steps["F2", k, g], steps["F3", k, g], steps["F4", k, g] = f1, second, third, f4

    steps["A",] = lambda: product(0, 0, 8)

    def b0():
        choose(1)
        product(1, 0, 2)

    steps["B", 0] = b0
    for i in range(1, 4):
        steps["B", i] = functools.partial(product, 1, 2 * i, 2 * i + 2)

    def s1():
        @pl.loop(0, 8)
        def _(i):
            at = pl.ds(pl.multiple_of(i * block, block), block)
            for h in range(2):
                value = full[2 * core + h, at, :]
                high = value.astype(BF16)
                s_v[at, 2 * h * width : (2 * h + 1) * width] = high
                s_v[at, (2 * h + 1) * width : (2 * h + 2) * width] = (value - high.astype(F32)).astype(BF16)

        q = lax.div(slab, 2)
        lane = lax.broadcasted_iota(jnp.int32, (width, width), 1)
        for k in range(CHUNKS):
            part = jnp.dot(wt[k], s_v[...], preferred_element_type=F32)
            even = part[:, :width] + part[:, width : 2 * width]
            odd = part[:, 2 * width : 3 * width] + part[:, 3 * width :]
            even = pltpu.roll(even, lax.rem(width - q * rows_q, width), 1)
            odd = pltpu.roll(odd, lax.rem(width + rows_q - q * rows_q, width), 1)
            mine = jnp.where(lane < rows_q, even, jnp.where(lane < 2 * rows_q, odd, 0.0))
            for o in range(8):
                sub_mine[o, k * rows_q : (k + 1) * rows_q, :] = mine[o * rows_q : (o + 1) * rows_q]
        for d in range(1, 8):
            links.send(("s", d), sub_mine.at[lax.rem(pair + d, 8)], sub_in.at[d - 1], peer(d))

    def s2():
        total = sub_mine[pair]
        for d in range(1, 8):
            links.wait(("s", d))
            total = total + sub_in[d - 1]
        square = jnp.concatenate([total, jnp.zeros_like(total)], axis=0)
        sub_out[...] = square.T[: 2 * rows_q, : 4 * rows_q]

    steps["S1",], steps["S2",] = s1, s2

    s_load.wait()
    choose(0)
    pl.semaphore_wait(barrier, len(greeted))
    assert sorted(ORDER, key=str) == sorted(steps, key=str)
    for name in ORDER:
        steps[name]()
    links.finish()
    for k in range(CHUNKS):
        for j in range(4):
            core_copy(k, j).wait_send()


def body(pair_density, subspace, band_valence, band_conduction, occupied, energies):
    pairs, depth = pair_density.shape
    nb = subspace.shape[1]
    total_pairs = pairs * lax.axis_size("pair")
    band_table = jnp.stack([energies, occupied.astype(F32)], axis=1)
    valence_rows = lookup(band_valence, band_table)
    conduction_rows = lookup(band_conduction, band_table)
    scale = 1.0 / math.sqrt(total_pairs)
    pair_weight = (
        -2.0
        * valence_rows[:, 1]
        * (1.0 - conduction_rows[:, 1])
        / (jnp.abs(conduction_rows[:, 0] - valence_rows[:, 0]) + 0.5)
        * scale
    )
    width, own, rows_q, cols = nb // CHUNKS, pairs // 16, nb // CHUNKS // 8, depth // PARTS
    copies = CHUNKS * (8 + 8 + 8) + CHUNKS * PARTS * 8 + 7
    vmem, dma = pltpu.VMEM, pltpu.SemaphoreType.DMA
    return pl.pallas_call(
        kernel,
        name="project",
        out_shape=(
            jax.ShapeDtypeStruct((nb // 8, depth), F32),
            jax.ShapeDtypeStruct((nb // 16, nb // 8), F32),
        ),
        in_specs=[
            pl.BlockSpec(memory_space=pl.ANY),
            pl.BlockSpec(memory_space=pl.ANY),
            pl.BlockSpec(memory_space=vmem),
        ],
        out_specs=(pl.BlockSpec(memory_space=vmem), pl.BlockSpec(memory_space=vmem)),
        scratch_shapes=[
            vmem((pairs, depth), BF16),
            vmem((depth, nb), BF16),
            vmem((depth, 2 * width), BF16),
            vmem((CHUNKS, pairs, width), F32),
            vmem((CHUNKS, pairs // 2, width), F32),
            vmem((CHUNKS, 8, own, width), F32),
            vmem((CHUNKS, pairs, width), F32),
            vmem((CHUNKS, width, pairs), BF16),
            vmem((CHUNKS, PARTS, width, cols), F32),
            vmem((CHUNKS, PARTS, 8, rows_q, cols), F32),
            vmem((8, nb // 8, width), F32),
            vmem((7, nb // 8, width), F32),
            dma((9,)),
            dma((CHUNKS, 4)),
            dma((CHUNKS, 4)),
            dma((copies,)),
            dma((copies,)),
        ],
        compiler_params=pltpu.CompilerParams(
            collective_id=0, has_side_effects=True, vmem_limit_bytes=67043328
        ),
    )(pair_density, subspace, pair_weight[None, :])


def solution(mesh):
    return jax.shard_map(
        body,
        mesh=mesh,
        in_specs=(P("pair", "slab"), P("slab", None), P("pair"), P("pair"), P(), P()),
        out_specs=(P("pair", "slab"), P("slab", "pair")),
        check_vma=False,
    )
```

```python
import functools
import math

import jax
import jax.numpy as jnp
from jax import lax
from jax.experimental import pallas as pl
from jax.experimental.pallas import tpu as pltpu
from jax.sharding import PartitionSpec as P

MESH = pl.DeviceIdType.MESH
F32, BF16 = jnp.float32, jnp.bfloat16

CHUNKS = 4
PARTS = 2
SUM_MODE = "BBBB"
SPREAD_MODE = "BABA"
PANEL_MODE = "BBBB"
ORDER = (
    ("A", 0), ("A", 1), ("A", 2), ("Q", 0, 0), ("Q", 0, 1), ("A", 3), ("Q", 0, 2), ("Q", 1, 0),
    ("Q", 1, 1), ("Q", 0, 3), ("R2", 0), ("Q", 1, 2), ("Q", 1, 3), ("B", 0), ("R3", 0), ("R2", 1),
    ("R5", 0), ("B", 1), ("R3", 1), ("R5", 1), ("B", 2), ("R4", 0), ("Q", 2, 0), ("R4", 1),
    ("B", 3), ("G2", 0), ("Q", 2, 1), ("G5", 0), ("L", 2), ("Q", 2, 2), ("G3", 0), ("G5", 1),
    ("Q", 2, 3), ("Q", 3, 0), ("L", 0), ("R2", 2), ("L", 1), ("Q", 3, 1), ("G4", 0), ("G2", 1),
    ("L", 3), ("Q", 3, 2), ("W", 0), ("R3", 2), ("G3", 1), ("Q", 3, 3), ("R2", 3), ("F1", 0, 0),
    ("R3", 3), ("R5", 2), ("F1", 0, 1), ("G4", 1), ("R5", 3), ("F2", 0, 0), ("R4", 2), ("W", 1),
    ("F1", 1, 0), ("G2", 2), ("G5", 2), ("F5", 0, 0), ("F2", 0, 1), ("R4", 3), ("G3", 2), ("F1", 1, 1),
    ("F2", 1, 0), ("G5", 3), ("G4", 2), ("G2", 3), ("F5", 0, 1), ("F3", 0, 0), ("G3", 3), ("W", 2),
    ("F5", 1, 0), ("F2", 1, 1), ("F3", 1, 0), ("F1", 2, 0), ("G4", 3), ("F1", 2, 1), ("F5", 1, 1), ("W", 3),
    ("F2", 2, 0), ("F3", 0, 1), ("F1", 3, 0), ("F3", 1, 1), ("F1", 3, 1), ("F2", 2, 1), ("F2", 3, 0), ("F4", 1, 0),
    ("F3", 2, 0), ("F5", 2, 0), ("S1",), ("F3", 3, 0), ("F4", 1, 1), ("F4", 0, 0), ("F2", 3, 1), ("F5", 2, 1),
    ("F3", 3, 1), ("F3", 2, 1), ("F5", 3, 1), ("F4", 0, 1), ("S2",), ("F5", 3, 0), ("F4", 3, 1), ("F4", 2, 1),
    ("F4", 2, 0), ("F4", 3, 0),
)


class Links:
    def __init__(self, send_sem, recv_sem):
        self.send_sem, self.recv_sem = send_sem, recv_sem
        self.made = {}

    def send(self, name, source, target, device):
        at = len(self.made)
        copy = pltpu.make_async_remote_copy(
            source, target, self.send_sem.at[at], self.recv_sem.at[at], device_id=device, device_id_type=MESH
        )
        copy.start()
        self.made[name] = copy

    def wait(self, *names):
        for name in names:
            self.made[name].wait_recv()

    def finish(self):
        for copy in self.made.values():
            copy.wait_send()


def ring_sum(links, tag, mode, piece, slots, ring_up, ring_down, across, half):
    lo, hi = pl.ds(0, half), pl.ds(half, half)

    def add(ref, *others):
        total = ref[...]
        for other in others:
            total = total + other[...]
        ref[...] = total

    def first(j):
        if mode == "B":
            if j == 0:
                links.send((tag, "y1"), piece(2, 1), slots.at[6], across)
            if j == 1:
                links.send((tag, "p1"), piece(1, 1), slots.at[0], ring_up)
            if j == 2:
                links.send((tag, "m1"), piece(3, 1), slots.at[1], ring_down)
        else:
            if j == 0:
                links.send((tag, "p2"), piece(2, 0), slots.at[2], ring_up)
                links.send((tag, "m2"), piece(2, 1), slots.at[3], ring_down)
            if j == 1:
                links.send((tag, "p1"), piece(1, 1), slots.at[0], ring_up)
            if j == 2:
                links.send((tag, "m1"), piece(3, 0), slots.at[1], ring_down)

    def second():
        if mode == "B":
            links.wait((tag, "y1"))
            add(piece(2, 0), slots.at[6])
            links.send((tag, "p2"), piece(2, 0).at[lo], slots.at[2, lo], ring_up)
            links.send((tag, "m2"), piece(2, 0).at[hi], slots.at[3, hi], ring_down)
        else:
            links.wait((tag, "p2"))
            add(piece(1, 0), slots.at[2])
            links.send((tag, "p3"), piece(1, 0), slots.at[4], ring_up)
            links.wait((tag, "m2"))
            add(piece(3, 1), slots.at[3])
            links.send((tag, "m3"), piece(3, 1), slots.at[5], ring_down)

    def third():
        if mode == "B":
            links.wait((tag, "p1"), (tag, "m1"))
            add(piece(0, 1), slots.at[0], slots.at[1])
            links.send((tag, "y3"), piece(0, 1), slots.at[7], across)
        else:
            links.wait((tag, "p1"), (tag, "m3"))
            add(piece(0, 1), slots.at[0], slots.at[5])
            links.send((tag, "y3"), piece(0, 1), slots.at[7], across)

    def fourth():
        links.wait((tag, "p2"))
        add(piece(1, 0).at[lo], slots.at[2, lo])
        links.send((tag, "p3"), piece(1, 0), slots.at[4], ring_up)
        links.wait((tag, "m2"))
        add(piece(3, 0).at[hi], slots.at[3, hi])
        links.send((tag, "m3"), piece(3, 0), slots.at[5], ring_down)

    def last():
        if mode == "B":
            links.wait((tag, "y3"), (tag, "p3"), (tag, "m3"))
            return piece(0, 0)[...] + slots[4] + slots[5] + slots[7]
        links.wait((tag, "m1"), (tag, "p3"), (tag, "y3"))
        return piece(0, 0)[...] + slots[1] + slots[4] + slots[7]

    return first, second, third, fourth, last


def kernel(
    a_hbm, s_hbm, valence_ref, conduction_ref, occupied_ref, energies_ref, chi_out, sub_out,
    w_ref, a_v, s_v, sp, coeff, core_in, sum_in, full, wt, chi, panel_in, sub_mine, sub_in,
    load_sem, core_send, core_recv, send_sem, recv_sem,
):
    pairs, depth = a_v.shape
    nb = s_v.shape[1]
    width = nb // CHUNKS
    block = pairs // 8
    own = block // 2
    rows_q = width // 8
    cols = depth // PARTS

    pair, slab = lax.axis_index("pair"), lax.axis_index("slab")
    y_hi, x = lax.div(pair, 4), lax.rem(pair, 4)
    y_lo, z, core = lax.div(slab, 8), lax.rem(lax.div(slab, 2), 4), lax.rem(slab, 2)

    def slab_of(y, zz, c):
        return (pair, y * 8 + zz * 2 + c)

    def pair_of(y, xx):
        return (y * 4 + xx, slab)

    def up(v, d):
        return lax.rem(v + d, 4)

    z_up, z_down = slab_of(y_lo, up(z, 1), core), slab_of(y_lo, up(z, 3), core)
    y_across, other_core = slab_of(1 - y_lo, z, core), slab_of(y_lo, z, 1 - core)
    x_up, x_down, hi_across = pair_of(y_hi, up(x, 1)), pair_of(y_hi, up(x, 3)), pair_of(1 - y_hi, x)

    def peer(d):
        return (lax.rem(pair + d, 8), slab)

    Z_ORDER = (2, 1, 3, 0)

    def block_rows(core_at, j):
        return pl.ds(pl.multiple_of((core_at * 4 + up(z, Z_ORDER[j])) * block, block), block)

    def half_rows(j):
        return pl.ds(pl.multiple_of(up(z, Z_ORDER[j]) * block, block), block)

    def side(i):
        return jnp.where(i == 0, 1 - core, core)

    def a_load(j, i):
        rows = block_rows(side(i), j)
        return pltpu.make_async_copy(a_hbm.at[rows], a_v.at[rows], load_sem.at[2 * j + i])

    s_load = pltpu.make_async_copy(s_hbm, s_v, load_sem.at[8])
    s_load.start()
    for j in range(4):
        for i in range(2):
            a_load(j, i).start()

    barrier = pltpu.get_barrier_semaphore()
    greeted = [z_up, z_down, y_across, other_core] + [peer(d) for d in range(1, 8)]
    for device in greeted:
        pl.semaphore_signal(barrier, inc=1, device_id=device, device_id_type=MESH)

    links = Links(send_sem, recv_sem)

    def choose(kp):
        to = lax.broadcasted_iota(jnp.int32, (nb, 2 * width), 1)
        frm = lax.broadcasted_iota(jnp.int32, (nb, 2 * width), 0)
        k = kp * 2 + to // width
        b = (lax.rem(to, width) // rows_q) * (nb // 8) + k * rows_q + lax.rem(to, rows_q)
        pick = jnp.where(frm == b, 1.0, 0.0).astype(BF16)

        @pl.loop(0, 8)
        def _(i):
            rows = pl.ds(pl.multiple_of(i * block, block), block)
            sp[rows, :] = jnp.dot(s_v[rows, :], pick, preferred_element_type=F32).astype(BF16)

    def core_copy(k, j):
        return pltpu.make_async_remote_copy(
            coeff.at[k, block_rows(1 - core, j)], core_in.at[k, half_rows(j)], core_send.at[k, j], core_recv.at[k, j],
            device_id=other_core, device_id_type=MESH,
        )

    def product(kp, j):
        @pl.loop(0, 2)
        def _(i):
            rows = block_rows(side(i), j)
            if kp == 0:
                a_load(j, i).wait()
            part = jnp.dot(a_v[rows, :], sp[...], preferred_element_type=F32)
            for h in range(2):
                coeff[2 * kp + h, rows, :] = part[:, h * width : (h + 1) * width]

            @pl.when(i == 0)
            def _():
                for h in range(2):
                    core_copy(2 * kp + h, j).start()

    def weights(j):
        at = slice(j * (pairs // 4), (j + 1) * (pairs // 4))
        bands = energies_ref.shape[1]
        energy = energies_ref[...]
        high = energy.astype(BF16).astype(F32)
        middle = (energy - high).astype(BF16).astype(F32)
        low = energy - high - middle
        row = lax.broadcasted_iota(jnp.int32, (16, bands), 0)
        table = jnp.where(row == 0, high, jnp.where(row == 1, middle, jnp.where(row == 2, low, 0.0)))
        table = jnp.where(row == 3, occupied_ref[...].astype(F32), table).astype(BF16)
        band = lax.broadcasted_iota(jnp.int32, (bands, pairs // 4), 0)

        def lookup(indices):
            one_hot = jnp.where(band == indices, 1.0, 0.0).astype(BF16)
            found = jnp.dot(table, one_hot, preferred_element_type=F32)
            return found[0:1] + found[1:2] + found[2:3], found[3:4]

        energy_low, filled_low = lookup(valence_ref[:, at])
        energy_high, filled_high = lookup(conduction_ref[:, at])
        scale = 1.0 / math.sqrt(pairs * 8)
        w_ref[:, at] = -2.0 * filled_low * (1.0 - filled_high) / (jnp.abs(energy_high - energy_low) + 0.5) * scale

    def owner_rows(z_at, y_at):
        return pl.ds(pl.multiple_of((core * 4 + z_at) * block + y_at * own, own), own)

    steps = {}
    for k in range(CHUNKS):
        get = lambda dr, da, k=k: coeff.at[k, owner_rows(up(z, dr), (1 - y_lo) if da else y_lo)]
        first, second, third, fourth, last = ring_sum(
            links, ("R", k), SUM_MODE[k], get, sum_in.at[k], z_up, z_down, y_across, own // 2
        )

        def gather(j, k=k, first=first):
            core_copy(k, j).wait_recv()
            here = block_rows(core, j)
            coeff[k, here, :] = coeff[k, here, :] + core_in[k, half_rows(j), :]
            first(j)

        for j in range(4):
            steps["Q", k, j] = functools.partial(gather, j)

        def spread(name, z_at, y_at, device, k=k, part=None):
            rows = owner_rows(z_at, y_at)
            if part is not None:
                start = (core * 4 + z_at) * block + y_at * own + part * (own // 2)
                rows = pl.ds(pl.multiple_of(start, own // 2), own // 2)
            links.send((name, k), full.at[k, rows], full.at[k, rows], device)

        def r4(k=k, last=last, spread=spread):
            full[k, owner_rows(z, y_lo), :] = last()
            spread("y1", z, y_lo, y_across)
            spread("p1", z, y_lo, z_up)
            spread("m1", z, y_lo, z_down)
            spread("c0", z, y_lo, other_core)

        whole = SPREAD_MODE[k] == "A"

        def g2(k=k, spread=spread, whole=whole):
            links.wait(("p1", k))
            spread("p2", up(z, 3), y_lo, z_up, part=None if whole else 0)
            links.wait(("m1", k))
            if not whole:
                spread("m2", up(z, 1), y_lo, z_down, part=1)
            spread("c1", up(z, 3), y_lo, other_core)
            spread("c2", up(z, 1), y_lo, other_core)

        def g5(k=k, spread=spread):
            links.wait(("y1", k))
            spread("p3", z, 1 - y_lo, z_up)
            spread("m3", z, 1 - y_lo, z_down)
            spread("c3", z, 1 - y_lo, other_core)

        def g3(k=k, spread=spread, whole=whole):
            if whole:
                links.wait(("m3", k))
                spread("m2", up(z, 1), 1 - y_lo, z_down)
                spread("c4", up(z, 1), 1 - y_lo, other_core)
            else:
                links.wait(("p2", k), ("m2", k))
                spread("y3", up(z, 2), y_lo, y_across)
                spread("c4", up(z, 2), y_lo, other_core)

        def g4(k=k, spread=spread, whole=whole):
            links.wait(("p3", k))
            spread("c5", up(z, 3), 1 - y_lo, other_core)
            if whole:
                links.wait(("p2", k))
                spread("c6", up(z, 2), y_lo, other_core)
                links.wait(("m2", k))
            else:
                links.wait(("m3", k))
                spread("c6", up(z, 1), 1 - y_lo, other_core)
                links.wait(("y3", k))
            spread("c7", up(z, 2), 1 - y_lo, other_core)

        def weigh(k=k):
            links.wait(*[(f"c{i}", k) for i in range(8)])

            @pl.loop(0, 8)
            def _(i):
                at = pl.ds(pl.multiple_of(i * block, block), block)
                wt[k, :, at] = (full[k, at, :].T * w_ref[:, at]).astype(BF16)

        steps["R2", k], steps["R3", k], steps["R4", k], steps["W", k] = second, third, r4, weigh
        steps["G2", k], steps["G5", k], steps["G3", k], steps["G4", k] = g2, g5, g3, g4
        if SUM_MODE[k] == "B":
            steps["R5", k] = fourth

        for g in range(PARTS):
            def rows_of(dx, dy, k=k, g=g):
                q = ((1 - y_hi) if dy else y_hi) * 4 + up(x, dx)
                return chi.at[k, g, pl.ds(pl.multiple_of(q * rows_q, rows_q), rows_q)]

            first, second, third, fourth, last = ring_sum(
                links, ("F", k, g), PANEL_MODE[k], rows_of, panel_in.at[k, g], x_up, x_down, hi_across, rows_q // 2
            )

            def f1(k=k, g=g, first=first):
                tile = cols // 3

                @pl.loop(0, 3)
                def _(i):
                    src = pl.ds(pl.multiple_of(g * cols + i * tile, tile), tile)
                    dst = pl.ds(pl.multiple_of(i * tile, tile), tile)
                    chi[k, g, :, dst] = jnp.dot(wt[k], a_v[:, src], preferred_element_type=F32)

                for j in range(3):
                    first(j)

            def f4(k=k, g=g, last=last):
                chi_out[k * rows_q : (k + 1) * rows_q, g * cols : (g + 1) * cols] = last()

            steps["F1", k, g], steps["F2", k, g], steps["F3", k, g], steps["F4", k, g] = f1, second, third, f4
            if PANEL_MODE[k] == "B":
                steps["F5", k, g] = fourth

    for j in range(4):
        steps["A", j] = functools.partial(product, 0, j)
        steps["L", j] = functools.partial(weights, j)
        steps["B", j] = functools.partial(product, 1, j)

    def b0():
        choose(1)
        product(1, 0)

    steps["B", 0] = b0

    def s1():
        @pl.loop(0, 8)
        def _(i):
            at = pl.ds(pl.multiple_of(i * block, block), block)
            for h in range(2):
                value = full[2 * core + h, at, :]
                high = value.astype(BF16)
                s_v[at, 2 * h * width : (2 * h + 1) * width] = high
                s_v[at, (2 * h + 1) * width : (2 * h + 2) * width] = (value - high.astype(F32)).astype(BF16)

        q = lax.div(slab, 2)
        lane = lax.broadcasted_iota(jnp.int32, (width, width), 1)
        for k in range(CHUNKS):
            part = jnp.dot(wt[k], s_v[...], preferred_element_type=F32)
            even = part[:, :width] + part[:, width : 2 * width]
            odd = part[:, 2 * width : 3 * width] + part[:, 3 * width :]
            even = pltpu.roll(even, lax.rem(width - q * rows_q, width), 1)
            odd = pltpu.roll(odd, lax.rem(width + rows_q - q * rows_q, width), 1)
            mine = jnp.where(lane < rows_q, even, jnp.where(lane < 2 * rows_q, odd, 0.0))
            for o in range(8):
                sub_mine[o, k * rows_q : (k + 1) * rows_q, :] = mine[o * rows_q : (o + 1) * rows_q]
        for d in range(1, 8):
            links.send(("s", d), sub_mine.at[lax.rem(pair + d, 8)], sub_in.at[d - 1], peer(d))

    def s2():
        total = sub_mine[pair]
        for d in range(1, 8):
            links.wait(("s", d))
            total = total + sub_in[d - 1]
        square = jnp.concatenate([total, jnp.zeros_like(total)], axis=0)
        sub_out[...] = square.T[: 2 * rows_q, : 4 * rows_q]

    steps["S1",], steps["S2",] = s1, s2

    s_load.wait()
    choose(0)
    pl.semaphore_wait(barrier, len(greeted))
    assert sorted(ORDER, key=str) == sorted(steps, key=str)
    for name in ORDER:
        steps[name]()
    links.finish()
    for k in range(CHUNKS):
        for j in range(4):
            core_copy(k, j).wait_send()


def hand_over(*arrays):
    parts = 4

    def kernel(*refs):
        sources, targets, held = refs[: len(arrays)], refs[len(arrays) : 2 * len(arrays)], refs[2 * len(arrays) : -1]
        sem = refs[-1]
        copies = []
        for n, (source, target, hold) in enumerate(zip(sources, targets, held)):
            rows = source.shape[0] // parts
            for i in range(parts):
                at = pl.ds(i * rows, rows)
                copies.append(
                    (
                        pltpu.make_async_copy(source.at[at], hold.at[at], sem.at[n, i, 0]),
                        pltpu.make_async_copy(hold.at[at], target.at[at], sem.at[n, i, 1]),
                    )
                )
        for load, _ in copies:
            load.start()
        for load, store in copies:
            load.wait()
            store.start()
        for _, store in copies:
            store.wait()

    return pl.pallas_call(
        kernel,
        name="hand_over",
        out_shape=tuple(jax.ShapeDtypeStruct(v.shape, v.dtype) for v in arrays),
        in_specs=[pl.BlockSpec(memory_space=pl.ANY)] * len(arrays),
        out_specs=tuple(pl.BlockSpec(memory_space=pl.ANY) for _ in arrays),
        scratch_shapes=[pltpu.VMEM(v.shape, v.dtype) for v in arrays]
        + [pltpu.SemaphoreType.DMA((len(arrays), parts, 2))],
    )(*arrays)


def body(pair_density, subspace, band_valence, band_conduction, occupied, energies):
    pairs, depth = pair_density.shape
    nb = subspace.shape[1]
    width, own, rows_q, cols = nb // CHUNKS, pairs // 16, nb // CHUNKS // 8, depth // PARTS
    copies = CHUNKS * (8 + 8 + 8) + CHUNKS * PARTS * 8 + 7
    vmem, dma = pltpu.VMEM, pltpu.SemaphoreType.DMA
    chi_panel, subspace_chi = pl.pallas_call(
        kernel,
        name="project",
        out_shape=(
            jax.ShapeDtypeStruct((nb // 8, depth), F32),
            jax.ShapeDtypeStruct((nb // 16, nb // 8), F32),
        ),
        in_specs=[
            pl.BlockSpec(memory_space=pl.ANY),
            pl.BlockSpec(memory_space=pl.ANY),
        ]
        + [pl.BlockSpec(memory_space=vmem)] * 4,
        out_specs=(pl.BlockSpec(memory_space=vmem), pl.BlockSpec(memory_space=vmem)),
        scratch_shapes=[
            vmem((1, pairs), F32),
            vmem((pairs, depth), BF16),
            vmem((depth, nb), BF16),
            vmem((depth, 2 * width), BF16),
            vmem((CHUNKS, pairs, width), F32),
            vmem((CHUNKS, pairs // 2, width), F32),
            vmem((CHUNKS, 8, own, width), F32),
            vmem((CHUNKS, pairs, width), F32),
            vmem((CHUNKS, width, pairs), BF16),
            vmem((CHUNKS, PARTS, width, cols), F32),
            vmem((CHUNKS, PARTS, 8, rows_q, cols), F32),
            vmem((8, nb // 8, width), F32),
            vmem((7, nb // 8, width), F32),
            dma((9,)),
            dma((CHUNKS, 4)),
            dma((CHUNKS, 4)),
            dma((copies,)),
            dma((copies,)),
        ],
        compiler_params=pltpu.CompilerParams(
            collective_id=0, has_side_effects=True, vmem_limit_bytes=67043328
        ),
    )(pair_density, subspace, band_valence[None, :], band_conduction[None, :], occupied[None, :], energies[None, :])
    return hand_over(chi_panel, subspace_chi)


def solution(mesh):
    return jax.shard_map(
        body,
        mesh=mesh,
        in_specs=(P("pair", "slab"), P("slab", None), P("pair"), P("pair"), P(), P()),
        out_specs=(P("pair", "slab"), P("slab", "pair")),
        check_vma=False,
    )
```

```python
import functools
import math

import jax
import jax.numpy as jnp
from jax import lax
from jax.experimental import pallas as pl
from jax.experimental.pallas import tpu as pltpu
from jax.sharding import PartitionSpec as P

MESH = pl.DeviceIdType.MESH
F32, BF16 = jnp.float32, jnp.bfloat16

CHUNKS = 4
PARTS = 2
SUM_MODE = "BABB"
SPREAD_MODE = "BBBB"
PANEL_MODE = "ABBBBBBB"
ORDER = (
    ("A", 0), ("A", 1), ("Q", 0, 0), ("Q", 1, 0), ("A", 2), ("Q", 0, 1), ("Q", 1, 1), ("Q", 0, 2),
    ("A", 3), ("Q", 0, 3), ("R2", 0), ("Q", 1, 2), ("B", 0), ("Q", 1, 3), ("R2", 1), ("B", 1),
    ("R3", 0), ("R5", 0), ("B", 2), ("Q", 2, 0), ("L", 1), ("Q", 2, 1), ("Q", 2, 2), ("L", 3),
    ("R3", 1), ("R4", 0), ("B", 3), ("R4", 1), ("Q", 3, 0), ("L", 0), ("G2", 0), ("L", 2),
    ("Q", 2, 3), ("G5", 0), ("R2", 2), ("G2", 1), ("G3", 0), ("Q", 3, 1), ("Q", 3, 2), ("Q", 3, 3),
    ("R2", 3), ("G5", 1), ("R3", 2), ("G4", 0), ("R5", 2), ("G3", 1), ("W", 0), ("F1", 0, 0),
    ("R3", 3), ("F1", 0, 1), ("R5", 3), ("G4", 1), ("W", 1), ("R4", 2), ("F1", 1, 0), ("R4", 3),
    ("F1", 1, 1), ("F2", 0, 1), ("G2", 2), ("G5", 2), ("F2", 0, 0), ("F2", 1, 0), ("G2", 3), ("G3", 2),
    ("F3", 1, 0), ("G5", 3), ("F5", 0, 1), ("F2", 1, 1), ("G3", 3), ("F3", 0, 0), ("G4", 2), ("F5", 1, 0),
    ("W", 2), ("F1", 2, 0), ("F5", 1, 1), ("G4", 3), ("F1", 2, 1), ("W", 3), ("F1", 3, 0), ("F1", 3, 1),
    ("F3", 0, 1), ("F3", 1, 1), ("S1",), ("F4", 0, 0), ("F2", 2, 0), ("F2", 2, 1), ("F2", 3, 0), ("F3", 2, 1),
    ("F2", 3, 1), ("F3", 3, 0), ("F3", 3, 1), ("F5", 2, 0), ("F5", 2, 1), ("S2",), ("F3", 2, 0), ("F5", 3, 1),
    ("F4", 1, 0), ("F5", 3, 0), ("F4", 2, 1), ("F4", 1, 1), ("F4", 2, 0), ("F4", 0, 1), ("F4", 3, 1), ("F4", 3, 0),
)


class Links:
    def __init__(self, send_sem, recv_sem, device):
        self.send_sem, self.recv_sem, self.device = send_sem, recv_sem, device
        self.sent, self.received, self.size = {}, {}, {}

    def send(self, send_group, group, source, target, device):
        out = self.sent.setdefault(send_group, len(self.sent))
        back = self.received.setdefault(group, len(self.received))
        pltpu.make_async_remote_copy(
            source, target, self.send_sem.at[out], self.recv_sem.at[back], device_id=device, device_id_type=MESH
        ).start()
        amount = math.prod(source.shape)
        self.size["s", send_group] = self.size.get(("s", send_group), 0) + amount
        self.size["r", group] = self.size.get(("r", group), 0) + amount

    def _all(self, kind, group, at, ref):
        assert math.prod(ref.shape) == self.size[kind, group], group
        return pltpu.make_async_remote_copy(
            ref, ref, self.send_sem.at[at if kind == "s" else 0], self.recv_sem.at[at if kind == "r" else 0],
            device_id=self.device, device_id_type=MESH,
        )

    def wait(self, group, ref):
        self._all("r", group, self.received[group], ref).wait_recv()

    def finish(self, group, ref):
        self._all("s", group, self.sent[group], ref).wait_send()


def ring_sum(links, tag, mode, piece, slots, ring_up, ring_down, across, half):
    lo, hi = pl.ds(0, half), pl.ds(half, half)

    def add(ref, *others):
        total = ref[...]
        for other in others:
            total = total + other[...]
        ref[...] = total

    def send(group, source, slot, device):
        links.send(tag, (tag, group), source, slot, device)

    def wait(group, ref):
        links.wait((tag, group), ref)

    def first(j):
        if mode == "B":
            if j == 0:
                send("a", piece(2, 1), slots.at[6], across)
            if j == 1:
                send("b", piece(1, 1), slots.at[0], ring_up)
            if j == 2:
                send("b", piece(3, 1), slots.at[1], ring_down)
        else:
            if j == 0:
                send("a", piece(2, 0), slots.at[2], ring_up)
                send("a", piece(2, 1), slots.at[3], ring_down)
            if j == 1:
                send("b", piece(1, 1), slots.at[0], ring_up)
            if j == 2:
                send("d", piece(3, 0), slots.at[1], ring_down)

    def second():
        if mode == "B":
            wait("a", slots.at[6])
            add(piece(2, 0), slots.at[6])
            send("c", piece(2, 0).at[lo], slots.at[2, lo], ring_up)
            send("c", piece(2, 0).at[hi], slots.at[3, hi], ring_down)
        else:
            wait("a", slots.at[pl.ds(2, 2)])
            add(piece(1, 0), slots.at[2])
            send("d", piece(1, 0), slots.at[4], ring_up)
            add(piece(3, 1), slots.at[3])
            send("b", piece(3, 1), slots.at[5], ring_down)

    def third():
        wait("b", slots.at[pl.ds(0, 2)])
        add(piece(0, 1), slots.at[0], slots.at[1 if mode == "B" else 5])
        send("d", piece(0, 1), slots.at[7], across)

    def fourth():
        wait("c", slots.at[2])
        add(piece(1, 0).at[lo], slots.at[2, lo])
        send("d", piece(1, 0), slots.at[4], ring_up)
        add(piece(3, 0).at[hi], slots.at[3, hi])
        send("d", piece(3, 0), slots.at[5], ring_down)

    def last():
        wait("d", slots.at[pl.ds(4, 3)])
        return piece(0, 0)[...] + slots[5 if mode == "B" else 1] + slots[4] + slots[7]

    return first, second, third, fourth, last


def kernel(
    a_hbm, s_hbm, valence_ref, conduction_ref, occupied_ref, energies_ref, chi_out, sub_out,
    w_ref, a_v, s_v, sp, coeff, core_in, sum_in, full, wt, chi, panel_in, sub_mine, sub_in,
    load_sem, core_send, core_recv, send_sem, recv_sem,
):
    pairs, depth = a_v.shape
    nb = s_v.shape[1]
    width = nb // CHUNKS
    block = pairs // 8
    own = block // 2
    rows_q = width // 8
    cols = depth // PARTS

    pair, slab = lax.axis_index("pair"), lax.axis_index("slab")
    y_hi, x = lax.div(pair, 4), lax.rem(pair, 4)
    y_lo, z, core = lax.div(slab, 8), lax.rem(lax.div(slab, 2), 4), lax.rem(slab, 2)

    def slab_of(y, zz, c):
        return (pair, y * 8 + zz * 2 + c)

    def pair_of(y, xx):
        return (y * 4 + xx, slab)

    def up(v, d):
        return lax.rem(v + d, 4)

    z_up, z_down = slab_of(y_lo, up(z, 1), core), slab_of(y_lo, up(z, 3), core)
    y_across, other_core = slab_of(1 - y_lo, z, core), slab_of(y_lo, z, 1 - core)
    x_up, x_down, hi_across = pair_of(y_hi, up(x, 1)), pair_of(y_hi, up(x, 3)), pair_of(1 - y_hi, x)

    def peer(d):
        return (lax.rem(pair + d, 8), slab)

    Z_ORDER = (2, 1, 3, 0)

    def block_rows(core_at, j):
        return pl.ds(pl.multiple_of((core_at * 4 + up(z, Z_ORDER[j])) * block, block), block)

    def half_rows(j):
        return pl.ds(pl.multiple_of(up(z, Z_ORDER[j]) * block, block), block)

    def side(i):
        return jnp.where(i == 0, 1 - core, core)

    def a_load(j, i):
        rows = block_rows(side(i), j)
        return pltpu.make_async_copy(a_hbm.at[rows], a_v.at[rows], load_sem.at[2 * j + i])

    barrier = pltpu.get_barrier_semaphore()
    greeted = [z_up, z_down, y_across, other_core] + [peer(d) for d in range(1, 8)]
    for device in greeted:
        pl.semaphore_signal(barrier, inc=1, device_id=device, device_id_type=MESH)

    def s_load(i):
        rows = pl.ds(pl.multiple_of(i * 2 * block, 2 * block), 2 * block)
        return pltpu.make_async_copy(s_hbm.at[rows], s_v.at[rows], load_sem.at[8 + i])

    for i in range(4):
        s_load(i).start()
    for j in range(4):
        for i in range(2):
            a_load(j, i).start()

    links = Links(send_sem, recv_sem, other_core)

    def pick(kp):
        to = lax.broadcasted_iota(jnp.int32, (1, 2 * width), 1)
        frm = lax.broadcasted_iota(jnp.int32, (nb, 2 * width), 0)
        k = kp * 2 + to // width
        b = (lax.rem(to, width) // rows_q) * (nb // 8) + k * rows_q + lax.rem(to, rows_q)
        return jnp.where(frm == b, 1.0, 0.0).astype(BF16)

    def choose(picked, loading):
        @pl.loop(0, 4)
        def _(i):
            if loading:
                s_load(i).wait()
            rows = pl.ds(pl.multiple_of(i * 2 * block, 2 * block), 2 * block)
            sp[rows, :] = jnp.dot(s_v[rows, :], picked, preferred_element_type=F32).astype(BF16)

    def core_copy(kp, j):
        two = pl.ds(2 * kp, 2)
        return pltpu.make_async_remote_copy(
            coeff.at[two, block_rows(1 - core, j)], core_in.at[two, half_rows(j)], core_send.at[kp], core_recv.at[kp, j],
            device_id=other_core, device_id_type=MESH,
        )

    def part_of_product(kp, j, i):
        rows = block_rows(side(i), j)
        if kp == 0:
            a_load(j, i).wait()
        part = jnp.dot(a_v[rows, :], sp[...], preferred_element_type=F32)
        for h in range(2):
            coeff[2 * kp + h, rows, :] = part[:, h * width : (h + 1) * width]

    def to_other_core(kp, j):
        core_copy(kp, j).start()

    def product(kp, j):
        @pl.loop(0, 2)
        def _(i):
            part_of_product(kp, j, i)

            @pl.when(i == 0)
            def _():
                to_other_core(kp, j)

    def weights(j):
        at = slice(j * (pairs // 4), (j + 1) * (pairs // 4))
        bands = energies_ref.shape[1]
        energy = energies_ref[...]
        high = energy.astype(BF16).astype(F32)
        middle = (energy - high).astype(BF16).astype(F32)
        low = energy - high - middle
        row = lax.broadcasted_iota(jnp.int32, (16, bands), 0)
        table = jnp.where(row == 0, high, jnp.where(row == 1, middle, jnp.where(row == 2, low, 0.0)))
        table = jnp.where(row == 3, occupied_ref[...].astype(F32), table).astype(BF16)
        band = lax.broadcasted_iota(jnp.int32, (bands, pairs // 4), 0)

        def lookup(indices):
            one_hot = jnp.where(band == indices, 1.0, 0.0).astype(BF16)
            found = jnp.dot(table, one_hot, preferred_element_type=F32)
            return found[0:1] + found[1:2] + found[2:3], found[3:4]

        energy_low, filled_low = lookup(valence_ref[:, at])
        energy_high, filled_high = lookup(conduction_ref[:, at])
        scale = 1.0 / math.sqrt(pairs * 8)
        w_ref[:, at] = -2.0 * filled_low * (1.0 - filled_high) / (jnp.abs(energy_high - energy_low) + 0.5) * scale

    def owner_rows(z_at, y_at):
        return pl.ds(pl.multiple_of((core * 4 + z_at) * block + y_at * own, own), own)

    steps = {}
    for k in range(CHUNKS):
        get = lambda dr, da, k=k: coeff.at[k, owner_rows(up(z, dr), (1 - y_lo) if da else y_lo)]
        first, second, third, fourth, last = ring_sum(
            links, ("R", k), SUM_MODE[k], get, sum_in.at[k], z_up, z_down, y_across, own // 2
        )

        def gather(j, k=k, first=first):
            if k % 2 == 0:
                core_copy(k // 2, j).wait_recv()
            here = block_rows(core, j)
            coeff[k, here, :] = coeff[k, here, :] + core_in[k, half_rows(j), :]
            first(j)

        for j in range(4):
            steps["Q", k, j] = functools.partial(gather, j)

        def spread(group, z_at, y_at, device, k=k, part=None):
            rows = owner_rows(z_at, y_at)
            if part is not None:
                start = (core * 4 + z_at) * block + y_at * own + part * (own // 2)
                rows = pl.ds(pl.multiple_of(start, own // 2), own // 2)
            links.send(("G", k), (group, k), full.at[k, rows], full.at[k, rows], device)

        def arrived(group, pieces, k=k):
            links.wait((group, k), full.at[k, pl.ds(0, pieces * own)])

        whole = SPREAD_MODE[k] == "A"

        def r4(k=k, last=last, spread=spread):
            full[k, owner_rows(z, y_lo), :] = last()
            spread("y", z, y_lo, y_across)
            spread("p", z, y_lo, z_up)
            spread("p", z, y_lo, z_down)
            spread("core", z, y_lo, other_core)

        def g2(spread=spread, arrived=arrived, whole=whole):
            arrived("p", 2)
            if whole:
                spread("l", up(z, 3), y_lo, z_up)
            else:
                spread("h", up(z, 3), y_lo, z_up, part=0)
                spread("h", up(z, 1), y_lo, z_down, part=1)
            spread("core", up(z, 3), y_lo, other_core)
            spread("core", up(z, 1), y_lo, other_core)

        def g5(spread=spread, arrived=arrived, whole=whole):
            arrived("y", 1)
            spread("l", z, 1 - y_lo, z_up)
            spread("h" if whole else "l", z, 1 - y_lo, z_down)
            spread("core", z, 1 - y_lo, other_core)

        def g3(spread=spread, arrived=arrived, whole=whole):
            arrived("h", 1)
            if whole:
                spread("l", up(z, 1), 1 - y_lo, z_down)
                spread("core", up(z, 1), 1 - y_lo, other_core)
            else:
                spread("l", up(z, 2), y_lo, y_across)
                spread("core", up(z, 2), y_lo, other_core)

        def weigh(core_at, k=k):
            for i in range(4):
                at = pl.ds(pl.multiple_of((core_at * 4 + i) * block, block), block)
                wt[k, :, at] = (full[k, at, :].T * w_ref[:, at]).astype(BF16)

        def g4(spread=spread, arrived=arrived, whole=whole, weigh=weigh):
            arrived("l", 3)
            spread("core", up(z, 3), 1 - y_lo, other_core)
            if whole:
                spread("core", up(z, 2), y_lo, other_core)
            else:
                spread("core", up(z, 1), 1 - y_lo, other_core)
            spread("core", up(z, 2), 1 - y_lo, other_core)
            weigh(core)

        def w1(arrived=arrived, weigh=weigh):
            arrived("core", 8)
            weigh(1 - core)

        steps["R2", k], steps["R3", k], steps["R4", k], steps["W", k] = second, third, r4, w1
        steps["G2", k], steps["G5", k], steps["G3", k], steps["G4", k] = g2, g5, g3, g4
        if SUM_MODE[k] == "B":
            steps["R5", k] = fourth

        for g in range(PARTS):
            def rows_of(dx, dy, k=k, g=g):
                q = ((1 - y_hi) if dy else y_hi) * 4 + up(x, dx)
                return chi.at[k, g, pl.ds(pl.multiple_of(q * rows_q, rows_q), rows_q)]

            first, second, third, fourth, last = ring_sum(
                links, ("F", k, g), PANEL_MODE[k * PARTS + g], rows_of, panel_in.at[k, g], x_up, x_down, hi_across, rows_q // 2
            )

            def f1(k=k, g=g, first=first):
                tile = cols // 3

                @pl.loop(0, 3)
                def _(i):
                    src = pl.ds(pl.multiple_of(g * cols + i * tile, tile), tile)
                    dst = pl.ds(pl.multiple_of(i * tile, tile), tile)
                    chi[k, g, :, dst] = jnp.dot(wt[k], a_v[:, src], preferred_element_type=F32)

                for j in range(3):
                    first(j)

            def f4(k=k, g=g, last=last):
                chi_out[k * rows_q : (k + 1) * rows_q, g * cols : (g + 1) * cols] = last()

            steps["F1", k, g], steps["F2", k, g], steps["F3", k, g], steps["F4", k, g] = f1, second, third, f4
            if PANEL_MODE[k * PARTS + g] == "B":
                steps["F5", k, g] = fourth

    for j in range(4):
        steps["A", j] = functools.partial(product, 0, j)
        steps["L", j] = functools.partial(weights, j)
        steps["B", j] = functools.partial(product, 1, j)

    def a0():
        part_of_product(0, 0, 0)
        pl.semaphore_wait(barrier, len(greeted))
        to_other_core(0, 0)
        part_of_product(0, 0, 1)

    def b0():
        choose(pick(1), False)
        product(1, 0)

    steps["A", 0], steps["B", 0] = a0, b0

    def s1():
        @pl.loop(0, 8)
        def _(i):
            at = pl.ds(pl.multiple_of(i * block, block), block)
            for h in range(2):
                value = full[2 * core + h, at, :]
                high = value.astype(BF16)
                s_v[at, 2 * h * width : (2 * h + 1) * width] = high
                s_v[at, (2 * h + 1) * width : (2 * h + 2) * width] = (value - high.astype(F32)).astype(BF16)

        q = lax.div(slab, 2)
        lane = lax.broadcasted_iota(jnp.int32, (width, width), 1)
        for k in range(CHUNKS):
            part = jnp.dot(wt[k], s_v[...], preferred_element_type=F32)
            even = part[:, :width] + part[:, width : 2 * width]
            odd = part[:, 2 * width : 3 * width] + part[:, 3 * width :]
            even = pltpu.roll(even, lax.rem(width - q * rows_q, width), 1)
            odd = pltpu.roll(odd, lax.rem(width + rows_q - q * rows_q, width), 1)
            mine = jnp.where(lane < rows_q, even, jnp.where(lane < 2 * rows_q, odd, 0.0))
            for o in range(8):
                sub_mine[o, k * rows_q : (k + 1) * rows_q, :] = mine[o * rows_q : (o + 1) * rows_q]
        for d in range(1, 8):
            links.send("s", "s", sub_mine.at[lax.rem(pair + d, 8)], sub_in.at[d - 1], peer(d))

    def s2():
        total = sub_mine[pair]
        links.wait("s", sub_in)
        for d in range(1, 8):
            total = total + sub_in[d - 1]
        square = jnp.concatenate([total, jnp.zeros_like(total)], axis=0)
        sub_out[...] = square.T[: 2 * rows_q, : 4 * rows_q]

    steps["S1",], steps["S2",] = s1, s2

    picked = pick(0)
    choose(picked, True)
    assert sorted(ORDER, key=str) == sorted(steps, key=str)
    for name in ORDER:
        steps[name]()
    for k in range(CHUNKS):
        links.finish(("R", k), sum_in.at[k, pl.ds(0, 7)])
        links.finish(("G", k), full.at[k, pl.ds(0, 15 * own)])
        for g in range(PARTS):
            links.finish(("F", k, g), panel_in.at[k, g, pl.ds(0, 7)])
    links.finish("s", sub_in)
    for kp in range(CHUNKS // 2):
        two = pl.ds(2 * kp, 2)
        pltpu.make_async_remote_copy(
            core_in.at[two], core_in.at[two], core_send.at[kp], core_recv.at[kp, 0],
            device_id=other_core, device_id_type=MESH,
        ).wait_send()


def hand_over(*arrays):
    def kernel(*refs):
        sources, targets, sem = refs[: len(arrays)], refs[len(arrays) : 2 * len(arrays)], refs[-1]
        copies = [
            pltpu.make_async_copy(source, target, sem.at[n])
            for n, (source, target) in enumerate(zip(sources, targets))
        ]
        for copy in copies:
            copy.start()
        for copy in copies:
            copy.wait()

    return pl.pallas_call(
        kernel,
        name="hand_over",
        out_shape=tuple(jax.ShapeDtypeStruct(v.shape, v.dtype) for v in arrays),
        in_specs=[pl.BlockSpec(memory_space=pltpu.VMEM)] * len(arrays),
        out_specs=tuple(pl.BlockSpec(memory_space=pl.ANY) for _ in arrays),
        scratch_shapes=[pltpu.SemaphoreType.DMA((len(arrays),))],
        compiler_params=pltpu.CompilerParams(vmem_limit_bytes=1 << 20),
    )(*arrays)


def body(pair_density, subspace, band_valence, band_conduction, occupied, energies):
    pairs, depth = pair_density.shape
    nb = subspace.shape[1]
    width, own, rows_q, cols = nb // CHUNKS, pairs // 16, nb // CHUNKS // 8, depth // PARTS
    vmem, dma = pltpu.VMEM, pltpu.SemaphoreType.DMA
    chi_panel, subspace_chi = pl.pallas_call(
        kernel,
        name="project",
        out_shape=(
            pltpu.VMEM((nb // 8, depth), F32),
            pltpu.VMEM((nb // 16, nb // 8), F32),
        ),
        in_specs=[
            pl.BlockSpec(memory_space=pl.ANY),
            pl.BlockSpec(memory_space=pl.ANY),
        ]
        + [pl.BlockSpec(memory_space=vmem)] * 4,
        out_specs=(pl.BlockSpec(memory_space=vmem), pl.BlockSpec(memory_space=vmem)),
        scratch_shapes=[
            vmem((1, pairs), F32),
            vmem((pairs, depth), BF16),
            vmem((depth, nb), BF16),
            vmem((depth, 2 * width), BF16),
            vmem((CHUNKS, pairs, width), F32),
            vmem((CHUNKS, pairs // 2, width), F32),
            vmem((CHUNKS, 8, own, width), F32),
            vmem((CHUNKS, pairs, width), F32),
            vmem((CHUNKS, width, pairs), BF16),
            vmem((CHUNKS, PARTS, width, cols), F32),
            vmem((CHUNKS, PARTS, 8, rows_q, cols), F32),
            vmem((8, nb // 8, width), F32),
            vmem((7, nb // 8, width), F32),
            dma((12,)),
            dma((CHUNKS // 2,)),
            dma((CHUNKS // 2, 4)),
            dma((CHUNKS * (2 + PARTS) + 1,)),
            dma((CHUNKS * (4 + 5) + CHUNKS * PARTS * 4 + 1,)),
        ],
        compiler_params=pltpu.CompilerParams(
            collective_id=0, has_side_effects=True, vmem_limit_bytes=62500000
        ),
    )(pair_density, subspace, band_valence[None, :], band_conduction[None, :], occupied[None, :], energies[None, :])
    return hand_over(chi_panel, subspace_chi)


def solution(mesh):
    return jax.shard_map(
        body,
        mesh=mesh,
        in_specs=(P("pair", "slab"), P("slab", None), P("pair"), P("pair"), P(), P()),
        out_specs=(P("pair", "slab"), P("slab", "pair")),
        check_vma=False,
    )
```

```python
import functools
import math

import jax
import jax.numpy as jnp
from jax import lax
from jax.experimental import pallas as pl
from jax.experimental.pallas import tpu as pltpu
from jax.sharding import PartitionSpec as P

MESH = pl.DeviceIdType.MESH
F32, BF16 = jnp.float32, jnp.bfloat16

CHUNKS = 4
TILE = 512
PARTS = 3
SUM_MODE = "BABB"
SPREAD_MODE = "BBBB"
PANEL_MODE = "BBABBBBBBBBB"
ORDER = (
    ("A", 0), ("A", 1), ("Q", 0, 0), ("Q", 1, 0), ("A", 2), ("L", 0), ("Q", 0, 1), ("Q", 0, 2),
    ("A", 3), ("Q", 0, 3), ("R2", 0), ("Q", 1, 1), ("Q", 1, 2), ("L", 2), ("Q", 1, 3), ("R2", 1),
    ("C",), ("B", 0), ("R5", 0), ("R3", 0), ("B", 1), ("Q", 2, 0), ("B", 2), ("Q", 2, 1),
    ("L", 3), ("Q", 2, 2), ("R3", 1), ("L", 1), ("R4", 0), ("B", 3), ("R4", 1), ("Q", 2, 3),
    ("R2", 2), ("G2", 0), ("G5", 0), ("Q", 3, 0), ("G2", 1), ("G5", 1), ("R5", 2), ("G3", 0),
    ("R3", 2), ("Q", 3, 1), ("Q", 3, 2), ("G4", 0), ("Q", 3, 3), ("V", 0), ("R2", 3), ("G3", 1),
    ("W", 0), ("F0", 0, 1, 0), ("F1", 0, 1), ("F0", 0, 2, 0), ("R4", 2), ("F1", 0, 2), ("G4", 1), ("V", 1),
    ("R3", 3), ("F0", 0, 0, 0), ("F1", 0, 0), ("R5", 3), ("W", 1), ("F0", 1, 1, 0), ("F1", 1, 1), ("G2", 2),
    ("F0", 1, 2, 0), ("F0", 1, 0, 0), ("F2", 0, 2), ("F2", 0, 1), ("F1", 1, 0), ("R4", 3), ("F1", 1, 2), ("G5", 2),
    ("F2", 1, 1), ("G3", 2), ("F2", 0, 0), ("F2", 1, 0), ("F3", 1, 0), ("F3", 0, 2), ("F5", 0, 1), ("G2", 3),
    ("F5", 1, 1), ("F2", 1, 2), ("G5", 3), ("F5", 0, 0), ("F5", 1, 0), ("G4", 2), ("G3", 3), ("V", 2),
    ("W", 2), ("F0", 2, 0, 0), ("F1", 2, 0), ("F0", 2, 2, 0), ("F5", 1, 2), ("F0", 2, 1, 0), ("F1", 2, 2), ("F1", 2, 1),
    ("G4", 3), ("V", 3), ("F3", 1, 1), ("W", 3), ("F0", 3, 2, 0), ("F1", 3, 2), ("F0", 3, 0, 0), ("F3", 0, 1),
    ("F2", 2, 2), ("F0", 3, 1, 0), ("F2", 2, 0), ("S0",), ("F1", 3, 1), ("F2", 2, 1), ("S", 0), ("F1", 3, 0),
    ("F3", 2, 2), ("S", 1), ("F3", 1, 2), ("S", 2), ("F3", 2, 1), ("F3", 2, 0), ("F4", 0, 2), ("F5", 2, 0),
    ("S", 3), ("F2", 3, 2), ("F4", 0, 1), ("F2", 3, 1), ("F4", 1, 1), ("S1",), ("F5", 2, 1), ("F2", 3, 0),
    ("F3", 3, 1), ("F3", 3, 0), ("S2",), ("F5", 2, 2), ("F3", 3, 2), ("F5", 3, 1), ("F4", 1, 0), ("F5", 3, 2),
    ("F5", 3, 0), ("S3",), ("F4", 2, 1), ("F3", 0, 0), ("S4",), ("F4", 1, 2), ("F4", 2, 2), ("F4", 2, 0),
    ("F4", 0, 0), ("F4", 3, 1), ("F4", 3, 2), ("F4", 3, 0),
)


class Links:
    def __init__(self, send_sem, recv_sem, device):
        self.send_sem, self.recv_sem, self.device = send_sem, recv_sem, device
        self.sent, self.received, self.size = {}, {}, {}

    def send(self, send_group, group, source, target, device):
        out = self.sent.setdefault(send_group, len(self.sent))
        back = self.received.setdefault(group, len(self.received))
        pltpu.make_async_remote_copy(
            source, target, self.send_sem.at[out], self.recv_sem.at[back], device_id=device, device_id_type=MESH
        ).start()
        amount = math.prod(source.shape)
        self.size["s", send_group] = self.size.get(("s", send_group), 0) + amount
        self.size["r", group] = self.size.get(("r", group), 0) + amount

    def _all(self, kind, group, at, ref):
        assert math.prod(ref.shape) == self.size[kind, group], group
        return pltpu.make_async_remote_copy(
            ref, ref, self.send_sem.at[at if kind == "s" else 0], self.recv_sem.at[at if kind == "r" else 0],
            device_id=self.device, device_id_type=MESH,
        )

    def wait(self, group, ref):
        self._all("r", group, self.received[group], ref).wait_recv()

    def finish(self, group, ref):
        self._all("s", group, self.sent[group], ref).wait_send()


def ring_sum(links, tag, mode, piece, slots, ring_up, ring_down, across, half):
    lo, hi = pl.ds(0, half), pl.ds(half, half)

    def add(ref, *others):
        total = ref[...]
        for other in others:
            total = total + other[...]
        ref[...] = total

    def send(group, source, slot, device):
        links.send(tag, (tag, group), source, slot, device)

    def wait(group, ref):
        links.wait((tag, group), ref)

    def first(j):
        if mode == "B":
            if j == 0:
                send("a", piece(2, 1), slots.at[6], across)
            if j == 1:
                send("b", piece(1, 1), slots.at[0], ring_up)
            if j == 2:
                send("b", piece(3, 1), slots.at[1], ring_down)
        else:
            if j == 0:
                send("a", piece(2, 0), slots.at[2], ring_up)
                send("a", piece(2, 1), slots.at[3], ring_down)
            if j == 1:
                send("b", piece(1, 1), slots.at[0], ring_up)
            if j == 2:
                send("d", piece(3, 0), slots.at[1], ring_down)

    def second():
        if mode == "B":
            wait("a", slots.at[6])
            add(piece(2, 0), slots.at[6])
            send("c", piece(2, 0).at[lo], slots.at[2, lo], ring_up)
            send("c", piece(2, 0).at[hi], slots.at[3, hi], ring_down)
        else:
            wait("a", slots.at[pl.ds(2, 2)])
            add(piece(1, 0), slots.at[2])
            send("d", piece(1, 0), slots.at[4], ring_up)
            add(piece(3, 1), slots.at[3])
            send("b", piece(3, 1), slots.at[5], ring_down)

    def third():
        wait("b", slots.at[pl.ds(0, 2)])
        add(piece(0, 1), slots.at[0], slots.at[1 if mode == "B" else 5])
        send("d", piece(0, 1), slots.at[7], across)

    def fourth():
        wait("c", slots.at[2])
        add(piece(1, 0).at[lo], slots.at[2, lo])
        send("d", piece(1, 0), slots.at[4], ring_up)
        add(piece(3, 0).at[hi], slots.at[3, hi])
        send("d", piece(3, 0), slots.at[5], ring_down)

    def last():
        wait("d", slots.at[pl.ds(4, 3)])
        return piece(0, 0)[...] + slots[5 if mode == "B" else 1] + slots[4] + slots[7]

    return first, second, third, fourth, last


def kernel(
    a_hbm, s_hbm, valence_ref, conduction_ref, occupied_ref, energies_ref, chi_out, sub_out,
    w_ref, a_v, s_v, sp, coeff, core_in, sum_in, full, wt, chi, panel_in, sub_mine, sub_in,
    load_sem, core_send, core_recv, send_sem, recv_sem,
):
    pairs, depth = a_v.shape
    nb = s_v.shape[1]
    width = nb // CHUNKS
    block = pairs // 8
    own = block // 2
    rows_q = width // 8
    cols = depth // PARTS

    pair, slab = lax.axis_index("pair"), lax.axis_index("slab")
    y_hi, x = lax.div(pair, 4), lax.rem(pair, 4)
    y_lo, z, core = lax.div(slab, 8), lax.rem(lax.div(slab, 2), 4), lax.rem(slab, 2)

    def slab_of(y, zz, c):
        return (pair, y * 8 + zz * 2 + c)

    def pair_of(y, xx):
        return (y * 4 + xx, slab)

    def up(v, d):
        return lax.rem(v + d, 4)

    z_up, z_down = slab_of(y_lo, up(z, 1), core), slab_of(y_lo, up(z, 3), core)
    y_across, other_core = slab_of(1 - y_lo, z, core), slab_of(y_lo, z, 1 - core)
    x_up, x_down, hi_across = pair_of(y_hi, up(x, 1)), pair_of(y_hi, up(x, 3)), pair_of(1 - y_hi, x)

    Z_ORDER = (2, 1, 3, 0)

    def block_rows(core_at, j):
        return pl.ds(pl.multiple_of((core_at * 4 + up(z, Z_ORDER[j])) * block, block), block)

    def half_rows(j):
        return pl.ds(pl.multiple_of(up(z, Z_ORDER[j]) * block, block), block)

    def side(i):
        return jnp.where(i == 0, 1 - core, core)

    def a_load(j, i):
        rows = block_rows(side(i), j)
        return pltpu.make_async_copy(a_hbm.at[rows], a_v.at[rows], load_sem.at[2 * j + i])

    barrier = pltpu.get_barrier_semaphore()
    greeted = [other_core, z_up, z_down, y_across, x_up, x_down, hi_across]
    for device in greeted:
        pl.semaphore_signal(barrier, inc=1, device_id=device, device_id_type=MESH)

    def s_load(i):
        rows = pl.ds(pl.multiple_of(i * 2 * block, 2 * block), 2 * block)
        return pltpu.make_async_copy(s_hbm.at[rows], s_v.at[rows], load_sem.at[8 + i])

    for i in range(4):
        s_load(i).start()
    for j in range(4):
        for i in range(2):
            a_load(j, i).start()

    links = Links(send_sem, recv_sem, other_core)

    def pick(kp):
        to = lax.broadcasted_iota(jnp.int32, (1, 2 * width), 1)
        frm = lax.broadcasted_iota(jnp.int32, (nb, 2 * width), 0)
        k = kp * 2 + to // width
        b = (lax.rem(to, width) // rows_q) * (nb // 8) + k * rows_q + lax.rem(to, rows_q)
        return jnp.where(frm == b, 1.0, 0.0).astype(BF16)

    def choose(picked, loading):
        @pl.loop(0, 4)
        def _(i):
            if loading:
                s_load(i).wait()
            rows = pl.ds(pl.multiple_of(i * 2 * block, 2 * block), 2 * block)
            sp[rows, :] = jnp.dot(s_v[rows, :], picked, preferred_element_type=F32).astype(BF16)

    def core_copy(kp, j):
        two = pl.ds(2 * kp, 2)
        return pltpu.make_async_remote_copy(
            coeff.at[two, block_rows(1 - core, j)], core_in.at[two, half_rows(j)], core_send.at[kp], core_recv.at[kp, j],
            device_id=other_core, device_id_type=MESH,
        )

    def part_of_product(kp, j, i):
        rows = block_rows(side(i), j)
        if kp == 0:
            a_load(j, i).wait()
        part = jnp.dot(a_v[rows, :], sp[...], preferred_element_type=F32)
        for h in range(2):
            coeff[2 * kp + h, rows, :] = part[:, h * width : (h + 1) * width]

    def to_other_core(kp, j):
        core_copy(kp, j).start()

    def product(kp, j):
        @pl.loop(0, 2)
        def _(i):
            part_of_product(kp, j, i)

            @pl.when(i == 0)
            def _():
                if kp == 0 and j == 0:
                    pl.semaphore_wait(barrier, len(greeted))
                to_other_core(kp, j)

    def weights(j):
        at = slice(j * (pairs // 4), (j + 1) * (pairs // 4))
        bands = energies_ref.shape[1]
        energy = energies_ref[...]
        high = energy.astype(BF16).astype(F32)
        middle = (energy - high).astype(BF16).astype(F32)
        low = energy - high - middle
        row = lax.broadcasted_iota(jnp.int32, (16, bands), 0)
        table = jnp.where(row == 0, high, jnp.where(row == 1, middle, jnp.where(row == 2, low, 0.0)))
        table = jnp.where(row == 3, occupied_ref[...].astype(F32), table).astype(BF16)
        band = lax.broadcasted_iota(jnp.int32, (bands, pairs // 4), 0)

        def lookup(indices):
            one_hot = jnp.where(band == indices, 1.0, 0.0).astype(BF16)
            found = jnp.dot(table, one_hot, preferred_element_type=F32)
            return found[0:1] + found[1:2] + found[2:3], found[3:4]

        energy_low, filled_low = lookup(valence_ref[:, at])
        energy_high, filled_high = lookup(conduction_ref[:, at])
        scale = 1.0 / math.sqrt(pairs * 8)
        w_ref[:, at] = -2.0 * filled_low * (1.0 - filled_high) / (jnp.abs(energy_high - energy_low) + 0.5) * scale

    def owner_rows(z_at, y_at):
        return pl.ds(pl.multiple_of((core * 4 + z_at) * block + y_at * own, own), own)

    steps = {}
    for k in range(CHUNKS):
        get = lambda dr, da, k=k: coeff.at[k, owner_rows(up(z, dr), (1 - y_lo) if da else y_lo)]
        first, second, third, fourth, last = ring_sum(
            links, ("R", k), SUM_MODE[k], get, sum_in.at[k], z_up, z_down, y_across, own // 2
        )

        def gather(j, k=k, first=first):
            if k % 2 == 0:
                core_copy(k // 2, j).wait_recv()
            here = block_rows(core, j)
            coeff[k, here, :] = coeff[k, here, :] + core_in[k, half_rows(j), :]
            first(j)

        for j in range(4):
            steps["Q", k, j] = functools.partial(gather, j)

        def spread(group, z_at, y_at, device, k=k, part=None):
            rows = owner_rows(z_at, y_at)
            if part is not None:
                start = (core * 4 + z_at) * block + y_at * own + part * (own // 2)
                rows = pl.ds(pl.multiple_of(start, own // 2), own // 2)
            links.send(("G", k), (group, k), full.at[k, rows], full.at[k, rows], device)

        def arrived(group, pieces, k=k):
            links.wait((group, k), full.at[k, pl.ds(0, pieces * own)])

        whole = SPREAD_MODE[k] == "A"

        def r4(k=k, last=last, spread=spread):
            full[k, owner_rows(z, y_lo), :] = last()
            spread("y", z, y_lo, y_across)
            spread("p", z, y_lo, z_up)
            spread("p", z, y_lo, z_down)
            spread("core", z, y_lo, other_core)

        def g2(spread=spread, arrived=arrived, whole=whole):
            arrived("p", 2)
            if whole:
                spread("l", up(z, 3), y_lo, z_up)
            else:
                spread("h", up(z, 3), y_lo, z_up, part=0)
                spread("h", up(z, 1), y_lo, z_down, part=1)
            spread("core", up(z, 3), y_lo, other_core)
            spread("core", up(z, 1), y_lo, other_core)

        def g5(spread=spread, arrived=arrived, whole=whole):
            arrived("y", 1)
            spread("l", z, 1 - y_lo, z_up)
            spread("h" if whole else "l", z, 1 - y_lo, z_down)
            spread("core", z, 1 - y_lo, other_core)

        def g3(spread=spread, arrived=arrived, whole=whole):
            arrived("h", 1)
            if whole:
                spread("l", up(z, 1), 1 - y_lo, z_down)
                spread("core", up(z, 1), 1 - y_lo, other_core)
            else:
                spread("l", up(z, 2), y_lo, y_across)
                spread("core", up(z, 2), y_lo, other_core)

        def weigh(core_at, k=k):
            for i in range(4):
                at = pl.ds(pl.multiple_of((core_at * 4 + i) * block, block), block)
                wt[k, :, at] = (full[k, at, :].T * w_ref[:, at]).astype(BF16)

        def g4(spread=spread, arrived=arrived, whole=whole):
            arrived("l", 3)
            spread("core", up(z, 3), 1 - y_lo, other_core)
            if whole:
                spread("core", up(z, 2), y_lo, other_core)
            else:
                spread("core", up(z, 1), 1 - y_lo, other_core)
            spread("core", up(z, 2), 1 - y_lo, other_core)

        def w1(arrived=arrived, weigh=weigh):
            arrived("core", 8)
            weigh(1 - core)

        steps["R2", k], steps["R3", k], steps["R4", k], steps["W", k] = second, third, r4, w1
        steps["G2", k], steps["G5", k], steps["G3", k], steps["G4", k] = g2, g5, g3, g4
        steps["V", k] = functools.partial(weigh, core)
        if SUM_MODE[k] == "B":
            steps["R5", k] = fourth

        for g in range(PARTS):
            def rows_of(dx, dy, k=k, g=g):
                q = ((1 - y_hi) if dy else y_hi) * 4 + up(x, dx)
                return chi.at[k, g, pl.ds(pl.multiple_of(q * rows_q, rows_q), rows_q)]

            first, second, third, fourth, last = ring_sum(
                links, ("F", k, g), PANEL_MODE[k * PARTS + g], rows_of, panel_in.at[k, g], x_up, x_down, hi_across, rows_q // 2
            )

            def tile(i, k=k, g=g):
                src, dst = pl.ds(g * cols + i * TILE, TILE), pl.ds(i * TILE, TILE)
                chi[k, g, :, dst] = jnp.dot(wt[k], a_v[:, src], preferred_element_type=F32)

            def f1(tile=tile, first=first):
                tile(cols // TILE - 1)
                for j in range(3):
                    first(j)

            for i in range(cols // TILE - 1):
                steps["F0", k, g, i] = functools.partial(tile, i)

            def f4(k=k, g=g, last=last):
                chi_out[k * rows_q : (k + 1) * rows_q, g * cols : (g + 1) * cols] = last()

            steps["F1", k, g], steps["F2", k, g], steps["F3", k, g], steps["F4", k, g] = f1, second, third, f4
            if PANEL_MODE[k * PARTS + g] == "B":
                steps["F5", k, g] = fourth

    for j in range(4):
        steps["A", j] = functools.partial(product, 0, j)
        steps["L", j] = functools.partial(weights, j)
        steps["B", j] = functools.partial(product, 1, j)
    steps["C",] = lambda: choose(pick(1), False)

    first, second, third, _, last = ring_sum(
        links, "S", "A",
        lambda dx, dy: sub_mine.at[((1 - y_hi) if dy else y_hi) * 4 + up(x, dx)],
        sub_in, x_up, x_down, hi_across, 0,
    )

    def s0():
        for i in range(8):
            at = pl.ds(i * block, block)
            for h in range(2):
                value = full[2 * core + h, at, :]
                high = value.astype(BF16)
                s_v[at, 2 * h * width : (2 * h + 1) * width] = high
                s_v[at, (2 * h + 1) * width : (2 * h + 2) * width] = (value - high.astype(F32)).astype(BF16)

    def s(k):
        q = lax.div(slab, 2)
        lane = lax.broadcasted_iota(jnp.int32, (width, width), 1)
        part = jnp.dot(wt[k], s_v[...], preferred_element_type=F32)
        even = part[:, :width] + part[:, width : 2 * width]
        odd = part[:, 2 * width : 3 * width] + part[:, 3 * width :]
        even = pltpu.roll(even, lax.rem(width - q * rows_q, width), 1)
        odd = pltpu.roll(odd, lax.rem(width + rows_q - q * rows_q, width), 1)
        mine = jnp.where(lane < rows_q, even, jnp.where(lane < 2 * rows_q, odd, 0.0))
        for o in range(8):
            sub_mine[o, k * rows_q : (k + 1) * rows_q, :] = mine[o * rows_q : (o + 1) * rows_q]

    def s1():
        for j in range(3):
            first(j)

    def s4():
        total = last()
        square = jnp.concatenate([total, jnp.zeros_like(total)], axis=0)
        sub_out[...] = square.T[: 2 * rows_q, : 4 * rows_q]

    steps["S0",], steps["S1",], steps["S2",], steps["S3",], steps["S4",] = s0, s1, second, third, s4
    for k in range(CHUNKS):
        steps["S", k] = functools.partial(s, k)

    picked = pick(0)
    choose(picked, True)
    assert sorted(ORDER, key=str) == sorted(steps, key=str)
    for name in ORDER:
        steps[name]()
    for k in range(CHUNKS):
        links.finish(("R", k), sum_in.at[k, pl.ds(0, 7)])
        links.finish(("G", k), full.at[k, pl.ds(0, 15 * own)])
        for g in range(PARTS):
            links.finish(("F", k, g), panel_in.at[k, g, pl.ds(0, 7)])
    links.finish("S", sub_in.at[pl.ds(0, 7)])
    for kp in range(CHUNKS // 2):
        two = pl.ds(2 * kp, 2)
        pltpu.make_async_remote_copy(
            core_in.at[two], core_in.at[two], core_send.at[kp], core_recv.at[kp, 0],
            device_id=other_core, device_id_type=MESH,
        ).wait_send()


def hand_over(*arrays):
    def kernel(*refs):
        sources, targets, sem = refs[: len(arrays)], refs[len(arrays) : 2 * len(arrays)], refs[-1]
        copies = [
            pltpu.make_async_copy(source, target, sem.at[n])
            for n, (source, target) in enumerate(zip(sources, targets))
        ]
        for copy in copies:
            copy.start()
        for copy in copies:
            copy.wait()

    return pl.pallas_call(
        kernel,
        name="hand_over",
        out_shape=tuple(jax.ShapeDtypeStruct(v.shape, v.dtype) for v in arrays),
        in_specs=[pl.BlockSpec(memory_space=pltpu.VMEM)] * len(arrays),
        out_specs=tuple(pl.BlockSpec(memory_space=pl.ANY) for _ in arrays),
        scratch_shapes=[pltpu.SemaphoreType.DMA((len(arrays),))],
        compiler_params=pltpu.CompilerParams(vmem_limit_bytes=1 << 20),
    )(*arrays)


def body(pair_density, subspace, band_valence, band_conduction, occupied, energies):
    pairs, depth = pair_density.shape
    nb = subspace.shape[1]
    width, own, rows_q, cols = nb // CHUNKS, pairs // 16, nb // CHUNKS // 8, depth // PARTS
    vmem, dma = pltpu.VMEM, pltpu.SemaphoreType.DMA
    chi_panel, subspace_chi = pl.pallas_call(
        kernel,
        name="project",
        out_shape=(
            pltpu.VMEM((nb // 8, depth), F32),
            pltpu.VMEM((nb // 16, nb // 8), F32),
        ),
        in_specs=[
            pl.BlockSpec(memory_space=pl.ANY),
            pl.BlockSpec(memory_space=pl.ANY),
        ]
        + [pl.BlockSpec(memory_space=vmem)] * 4,
        out_specs=(pl.BlockSpec(memory_space=vmem), pl.BlockSpec(memory_space=vmem)),
        scratch_shapes=[
            vmem((1, pairs), F32),
            vmem((pairs, depth), BF16),
            vmem((depth, nb), BF16),
            vmem((depth, 2 * width), BF16),
            vmem((CHUNKS, pairs, width), F32),
            vmem((CHUNKS, pairs // 2, width), F32),
            vmem((CHUNKS, 8, own, width), F32),
            vmem((CHUNKS, pairs, width), F32),
            vmem((CHUNKS, width, pairs), BF16),
            vmem((CHUNKS, PARTS, width, cols), F32),
            vmem((CHUNKS, PARTS, 8, rows_q, cols), F32),
            vmem((8, nb // 8, width), F32),
            vmem((8, nb // 8, width), F32),
            dma((12,)),
            dma((CHUNKS // 2,)),
            dma((CHUNKS // 2, 4)),
            dma((CHUNKS * (2 + PARTS) + 1,)),
            dma((CHUNKS * (4 + 5) + CHUNKS * PARTS * 4 + 3,)),
        ],
        compiler_params=pltpu.CompilerParams(
            collective_id=0, has_side_effects=True, vmem_limit_bytes=62500000
        ),
    )(pair_density, subspace, band_valence[None, :], band_conduction[None, :], occupied[None, :], energies[None, :])
    return hand_over(chi_panel, subspace_chi)


def solution(mesh):
    return jax.shard_map(
        body,
        mesh=mesh,
        in_specs=(P("pair", "slab"), P("slab", None), P("pair"), P("pair"), P(), P()),
        out_specs=(P("pair", "slab"), P("slab", "pair")),
        check_vma=False,
    )
```

```python
import functools
import math

import jax
import jax.numpy as jnp
from jax import lax
from jax.experimental import pallas as pl
from jax.experimental.pallas import tpu as pltpu
from jax.sharding import PartitionSpec as P

MESH = pl.DeviceIdType.MESH
F32, BF16 = jnp.float32, jnp.bfloat16

CHUNKS = 4
TILE = 512
PARTS = 3
SUM_MODE = "BABB"
SPREAD_MODE = "BBAB"
PANEL_MODE = "BBABBBBBBBBB"
ORDER = (
    ("A", 0), ("A", 1), ("Q", 0, 0), ("Q", 1, 0), ("A", 2), ("L", 1), ("Q", 0, 1), ("Q", 0, 2),
    ("A", 3), ("Q", 0, 3), ("R2", 0), ("Q", 1, 1), ("Q", 1, 2), ("C",), ("B", 0), ("R3", 0),
    ("Q", 1, 3), ("R5", 0), ("R2", 1), ("L", 0), ("Q", 2, 0), ("B", 1), ("B", 2), ("R4", 0),
    ("B", 3), ("Q", 2, 1), ("Q", 2, 2), ("R3", 1), ("Q", 2, 3), ("Q", 3, 0), ("R2", 2), ("L", 2),
    ("L", 3), ("G2", 0), ("R4", 1), ("G5", 0), ("G3", 0), ("G2", 1), ("R5", 2), ("G5", 1),
    ("Q", 3, 1), ("R3", 2), ("G4", 0), ("V", 0), ("W", 0), ("G3", 1), ("F0", 0, 2, 0), ("F1", 0, 2),
    ("Q", 3, 2), ("Q", 3, 3), ("R2", 3), ("F0", 0, 1, 0), ("F1", 0, 1), ("F0", 0, 0, 0), ("R4", 2), ("F1", 0, 0),
    ("G4", 1), ("F2", 0, 2), ("V", 1), ("W", 1), ("R3", 3), ("F0", 1, 1, 0), ("R5", 3), ("F2", 0, 1),
    ("F0", 1, 2, 0), ("F1", 1, 1), ("F0", 1, 0, 0), ("G5", 2), ("F1", 1, 2), ("F1", 1, 0), ("F2", 0, 0), ("R4", 3),
    ("F2", 1, 1), ("F3", 0, 1), ("G2", 2), ("G3", 2), ("F5", 0, 1), ("F2", 1, 2), ("F2", 1, 0), ("F5", 0, 0),
    ("G2", 3), ("F5", 1, 1), ("F3", 1, 0), ("G5", 3), ("G4", 2), ("F3", 1, 1), ("V", 2), ("F5", 1, 2),
    ("W", 2), ("F5", 1, 0), ("G3", 3), ("F0", 2, 1, 0), ("F0", 2, 0, 0), ("F1", 2, 0), ("F1", 2, 1), ("F0", 2, 2, 0),
    ("F1", 2, 2), ("G4", 3), ("F3", 1, 2), ("V", 3), ("W", 3), ("F0", 3, 0, 0), ("F2", 2, 0), ("F1", 3, 0),
    ("F0", 3, 2, 0), ("F1", 3, 2), ("F0", 3, 1, 0), ("F1", 3, 1), ("F3", 2, 0), ("S0",), ("F4", 1, 0), ("F5", 2, 0),
    ("F2", 3, 0), ("F3", 3, 0), ("F2", 2, 2), ("F2", 2, 1), ("F2", 3, 2), ("S", 0), ("S", 1), ("F3", 2, 2),
    ("F2", 3, 1), ("S", 2), ("F3", 0, 0), ("F3", 2, 1), ("F3", 3, 1), ("S", 3), ("S1",), ("F5", 2, 1),
    ("F5", 2, 2), ("S2",), ("F5", 3, 0), ("F5", 3, 1), ("F3", 0, 2), ("F4", 0, 0), ("F3", 3, 2), ("F5", 3, 2),
    ("S3",), ("F4", 2, 2), ("F4", 1, 2), ("F4", 2, 1), ("F4", 2, 0), ("F4", 3, 0), ("F4", 0, 1), ("F4", 1, 1),
    ("F4", 3, 1), ("S4",), ("F4", 0, 2), ("F4", 3, 2),
)


class Links:
    def __init__(self, send_sem, recv_sem, device):
        self.send_sem, self.recv_sem, self.device = send_sem, recv_sem, device
        self.sent, self.received, self.size = {}, {}, {}

    def send(self, send_group, group, source, target, device):
        out = self.sent.setdefault(send_group, len(self.sent))
        back = self.received.setdefault(group, len(self.received))
        pltpu.make_async_remote_copy(
            source, target, self.send_sem.at[out], self.recv_sem.at[back], device_id=device, device_id_type=MESH
        ).start()
        amount = math.prod(source.shape)
        self.size["s", send_group] = self.size.get(("s", send_group), 0) + amount
        self.size["r", group] = self.size.get(("r", group), 0) + amount

    def _all(self, kind, group, at, ref):
        assert math.prod(ref.shape) == self.size[kind, group], group
        return pltpu.make_async_remote_copy(
            ref, ref, self.send_sem.at[at if kind == "s" else 0], self.recv_sem.at[at if kind == "r" else 0],
            device_id=self.device, device_id_type=MESH,
        )

    def wait(self, group, ref):
        self._all("r", group, self.received[group], ref).wait_recv()

    def finish(self, group, ref):
        self._all("s", group, self.sent[group], ref).wait_send()


def ring_sum(links, tag, mode, piece, slots, ring_up, ring_down, across, half):
    lo, hi = pl.ds(0, half), pl.ds(half, half)

    def add(ref, *others):
        total = ref[...]
        for other in others:
            total = total + other[...]
        ref[...] = total

    def send(group, source, slot, device):
        links.send(tag, (tag, group), source, slot, device)

    def wait(group, ref):
        links.wait((tag, group), ref)

    def first(j):
        if mode == "B":
            if j == 0:
                send("a", piece(2, 1), slots.at[6], across)
            if j == 1:
                send("b", piece(1, 1), slots.at[0], ring_up)
            if j == 2:
                send("b", piece(3, 1), slots.at[1], ring_down)
        else:
            if j == 0:
                send("a", piece(2, 0), slots.at[2], ring_up)
                send("a", piece(2, 1), slots.at[3], ring_down)
            if j == 1:
                send("b", piece(1, 1), slots.at[0], ring_up)
            if j == 2:
                send("d", piece(3, 0), slots.at[1], ring_down)

    def second():
        if mode == "B":
            wait("a", slots.at[6])
            add(piece(2, 0), slots.at[6])
            send("c", piece(2, 0).at[lo], slots.at[2, lo], ring_up)
            send("c", piece(2, 0).at[hi], slots.at[3, hi], ring_down)
        else:
            wait("a", slots.at[pl.ds(2, 2)])
            add(piece(1, 0), slots.at[2])
            send("d", piece(1, 0), slots.at[4], ring_up)
            add(piece(3, 1), slots.at[3])
            send("b", piece(3, 1), slots.at[5], ring_down)

    def third():
        wait("b", slots.at[pl.ds(0, 2)])
        add(piece(0, 1), slots.at[0], slots.at[1 if mode == "B" else 5])
        send("d", piece(0, 1), slots.at[7], across)

    def fourth():
        wait("c", slots.at[2])
        add(piece(1, 0).at[lo], slots.at[2, lo])
        send("d", piece(1, 0), slots.at[4], ring_up)
        add(piece(3, 0).at[hi], slots.at[3, hi])
        send("d", piece(3, 0), slots.at[5], ring_down)

    def last():
        wait("d", slots.at[pl.ds(4, 3)])
        return piece(0, 0)[...] + slots[5 if mode == "B" else 1] + slots[4] + slots[7]

    return first, second, third, fourth, last


def kernel(
    a_hbm, s_hbm, valence_ref, conduction_ref, occupied_ref, energies_ref, chi_out, sub_out,
    w_ref, a_v, s_v, sp, coeff, core_in, sum_in, full, wt, chi, panel_in, sub_mine, sub_in,
    load_sem, core_send, core_recv, send_sem, recv_sem,
):
    pairs, depth = a_v.shape
    nb = s_v.shape[1]
    width = nb // CHUNKS
    block = pairs // 8
    own = block // 2
    rows_q = width // 8
    cols = depth // PARTS

    pair, slab = lax.axis_index("pair"), lax.axis_index("slab")
    y_hi, x = lax.div(pair, 4), lax.rem(pair, 4)
    y_lo, z, core = lax.div(slab, 8), lax.rem(lax.div(slab, 2), 4), lax.rem(slab, 2)

    def slab_of(y, zz, c):
        return (pair, y * 8 + zz * 2 + c)

    def pair_of(y, xx):
        return (y * 4 + xx, slab)

    def up(v, d):
        return lax.rem(v + d, 4)

    z_up, z_down = slab_of(y_lo, up(z, 1), core), slab_of(y_lo, up(z, 3), core)
    y_across, other_core = slab_of(1 - y_lo, z, core), slab_of(y_lo, z, 1 - core)
    x_up, x_down, hi_across = pair_of(y_hi, up(x, 1)), pair_of(y_hi, up(x, 3)), pair_of(1 - y_hi, x)

    Z_ORDER = (2, 1, 3, 0)

    def block_rows(core_at, j):
        return pl.ds(pl.multiple_of((core_at * 4 + up(z, Z_ORDER[j])) * block, block), block)

    def half_rows(j):
        return pl.ds(pl.multiple_of(up(z, Z_ORDER[j]) * block, block), block)

    def side(i):
        return jnp.where(i == 0, 1 - core, core)

    def a_load(j, i):
        rows = block_rows(side(i), j)
        return pltpu.make_async_copy(a_hbm.at[rows], a_v.at[rows], load_sem.at[2 * j + i])

    barrier = pltpu.get_barrier_semaphore()
    greeted = [other_core, z_up, z_down, y_across, x_up, x_down, hi_across]
    for device in greeted:
        pl.semaphore_signal(barrier, inc=1, device_id=device, device_id_type=MESH)

    def s_load(i):
        rows = pl.ds(pl.multiple_of(i * 2 * block, 2 * block), 2 * block)
        return pltpu.make_async_copy(s_hbm.at[rows], s_v.at[rows], load_sem.at[8 + i])

    for i in range(4):
        s_load(i).start()
    for j in range(4):
        for i in range(2):
            a_load(j, i).start()

    links = Links(send_sem, recv_sem, other_core)

    def pick(kp):
        to = lax.broadcasted_iota(jnp.int32, (1, 2 * width), 1)
        frm = lax.broadcasted_iota(jnp.int32, (nb, 2 * width), 0)
        k = kp * 2 + to // width
        b = (lax.rem(to, width) // rows_q) * (nb // 8) + k * rows_q + lax.rem(to, rows_q)
        return jnp.where(frm == b, 1.0, 0.0).astype(BF16)

    def choose(picked, loading):
        @pl.loop(0, 4)
        def _(i):
            if loading:
                s_load(i).wait()
            rows = pl.ds(pl.multiple_of(i * 2 * block, 2 * block), 2 * block)
            sp[rows, :] = jnp.dot(s_v[rows, :], picked, preferred_element_type=F32).astype(BF16)

    def core_copy(kp, j):
        two = pl.ds(2 * kp, 2)
        return pltpu.make_async_remote_copy(
            coeff.at[two, block_rows(1 - core, j)], core_in.at[two, half_rows(j)], core_send.at[kp], core_recv.at[kp, j],
            device_id=other_core, device_id_type=MESH,
        )

    def part_of_product(kp, j, i):
        rows = block_rows(side(i), j)
        if kp == 0:
            a_load(j, i).wait()
        part = jnp.dot(a_v[rows, :], sp[...], preferred_element_type=F32)
        for h in range(2):
            coeff[2 * kp + h, rows, :] = part[:, h * width : (h + 1) * width]

    def to_other_core(kp, j):
        core_copy(kp, j).start()

    def product(kp, j):
        @pl.loop(0, 2)
        def _(i):
            part_of_product(kp, j, i)

            @pl.when(i == 0)
            def _():
                if kp == 0 and j == 0:
                    pl.semaphore_wait(barrier, len(greeted))
                to_other_core(kp, j)

    def weights(j):
        at = slice(j * (pairs // 4), (j + 1) * (pairs // 4))
        bands = energies_ref.shape[1]
        energy = energies_ref[...]
        high = energy.astype(BF16).astype(F32)
        middle = (energy - high).astype(BF16).astype(F32)
        low = energy - high - middle
        row = lax.broadcasted_iota(jnp.int32, (16, bands), 0)
        table = jnp.where(row == 0, high, jnp.where(row == 1, middle, jnp.where(row == 2, low, 0.0)))
        table = jnp.where(row == 3, occupied_ref[...].astype(F32), table).astype(BF16)
        band = lax.broadcasted_iota(jnp.int32, (bands, pairs // 4), 0)

        def lookup(indices):
            one_hot = jnp.where(band == indices, 1.0, 0.0).astype(BF16)
            found = jnp.dot(table, one_hot, preferred_element_type=F32)
            return found[0:1] + found[1:2] + found[2:3], found[3:4]

        energy_low, filled_low = lookup(valence_ref[:, at])
        energy_high, filled_high = lookup(conduction_ref[:, at])
        scale = 1.0 / math.sqrt(pairs * 8)
        w_ref[:, at] = -2.0 * filled_low * (1.0 - filled_high) / (jnp.abs(energy_high - energy_low) + 0.5) * scale

    def owner_rows(z_at, y_at):
        return pl.ds(pl.multiple_of((core * 4 + z_at) * block + y_at * own, own), own)

    steps = {}
    for k in range(CHUNKS):
        get = lambda dr, da, k=k: coeff.at[k, owner_rows(up(z, dr), (1 - y_lo) if da else y_lo)]
        first, second, third, fourth, last = ring_sum(
            links, ("R", k), SUM_MODE[k], get, sum_in.at[k], z_up, z_down, y_across, own // 2
        )

        def gather(j, k=k, first=first):
            if k % 2 == 0:
                core_copy(k // 2, j).wait_recv()
            here = block_rows(core, j)
            coeff[k, here, :] = coeff[k, here, :] + core_in[k, half_rows(j), :]
            first(j)

        for j in range(4):
            steps["Q", k, j] = functools.partial(gather, j)

        def spread(group, z_at, y_at, device, k=k, part=None):
            rows = owner_rows(z_at, y_at)
            if part is not None:
                start = (core * 4 + z_at) * block + y_at * own + part * (own // 2)
                rows = pl.ds(pl.multiple_of(start, own // 2), own // 2)
            links.send(("G", k), (group, k), full.at[k, rows], full.at[k, rows], device)

        def arrived(group, pieces, k=k):
            links.wait((group, k), full.at[k, pl.ds(0, pieces * own)])

        whole = SPREAD_MODE[k] == "A"

        def r4(k=k, last=last, spread=spread):
            full[k, owner_rows(z, y_lo), :] = last()
            spread("y", z, y_lo, y_across)
            spread("p", z, y_lo, z_up)
            spread("p", z, y_lo, z_down)
            spread("core", z, y_lo, other_core)

        def g2(spread=spread, arrived=arrived, whole=whole):
            arrived("p", 2)
            if whole:
                spread("l", up(z, 3), y_lo, z_up)
            else:
                spread("h", up(z, 3), y_lo, z_up, part=0)
                spread("h", up(z, 1), y_lo, z_down, part=1)
            spread("core", up(z, 3), y_lo, other_core)
            spread("core", up(z, 1), y_lo, other_core)

        def g5(spread=spread, arrived=arrived, whole=whole):
            arrived("y", 1)
            spread("l", z, 1 - y_lo, z_up)
            spread("h" if whole else "l", z, 1 - y_lo, z_down)
            spread("core", z, 1 - y_lo, other_core)

        def g3(spread=spread, arrived=arrived, whole=whole):
            arrived("h", 1)
            if whole:
                spread("l", up(z, 1), 1 - y_lo, z_down)
                spread("core", up(z, 1), 1 - y_lo, other_core)
            else:
                spread("l", up(z, 2), y_lo, y_across)
                spread("core", up(z, 2), y_lo, other_core)

        def weigh(core_at, k=k):
            for i in range(4):
                at = pl.ds(pl.multiple_of((core_at * 4 + i) * block, block), block)
                wt[k, :, at] = (full[k, at, :].T * w_ref[:, at]).astype(BF16)

        def g4(spread=spread, arrived=arrived, whole=whole):
            arrived("l", 3)
            spread("core", up(z, 3), 1 - y_lo, other_core)
            if whole:
                spread("core", up(z, 2), y_lo, other_core)
            else:
                spread("core", up(z, 1), 1 - y_lo, other_core)
            spread("core", up(z, 2), 1 - y_lo, other_core)

        def w1(arrived=arrived, weigh=weigh):
            arrived("core", 8)
            weigh(1 - core)

        steps["R2", k], steps["R3", k], steps["R4", k], steps["W", k] = second, third, r4, w1
        steps["G2", k], steps["G5", k], steps["G3", k], steps["G4", k] = g2, g5, g3, g4
        steps["V", k] = functools.partial(weigh, core)
        if SUM_MODE[k] == "B":
            steps["R5", k] = fourth

        for g in range(PARTS):
            def rows_of(dx, dy, k=k, g=g):
                q = ((1 - y_hi) if dy else y_hi) * 4 + up(x, dx)
                return chi.at[k, g, pl.ds(pl.multiple_of(q * rows_q, rows_q), rows_q)]

            first, second, third, fourth, last = ring_sum(
                links, ("F", k, g), PANEL_MODE[k * PARTS + g], rows_of, panel_in.at[k, g], x_up, x_down, hi_across, rows_q // 2
            )

            def tile(i, k=k, g=g):
                src, dst = pl.ds(g * cols + i * TILE, TILE), pl.ds(i * TILE, TILE)
                chi[k, g, :, dst] = jnp.dot(wt[k], a_v[:, src], preferred_element_type=F32)

            def f1(tile=tile, first=first):
                tile(cols // TILE - 1)
                for j in range(3):
                    first(j)

            for i in range(cols // TILE - 1):
                steps["F0", k, g, i] = functools.partial(tile, i)

            def f4(k=k, g=g, last=last):
                chi_out[k * rows_q : (k + 1) * rows_q, g * cols : (g + 1) * cols] = last()

            steps["F1", k, g], steps["F2", k, g], steps["F3", k, g], steps["F4", k, g] = f1, second, third, f4
            if PANEL_MODE[k * PARTS + g] == "B":
                steps["F5", k, g] = fourth

    for j in range(4):
        steps["A", j] = functools.partial(product, 0, j)
        steps["L", j] = functools.partial(weights, j)
        steps["B", j] = functools.partial(product, 1, j)
    steps["C",] = lambda: choose(pick(1), False)

    first, second, third, _, last = ring_sum(
        links, "S", "A",
        lambda dx, dy: sub_mine.at[((1 - y_hi) if dy else y_hi) * 4 + up(x, dx)],
        sub_in, x_up, x_down, hi_across, 0,
    )

    def s0():
        for i in range(8):
            at = pl.ds(i * block, block)
            for h in range(2):
                value = full[2 * core + h, at, :]
                high = value.astype(BF16)
                s_v[at, 2 * h * width : (2 * h + 1) * width] = high
                s_v[at, (2 * h + 1) * width : (2 * h + 2) * width] = (value - high.astype(F32)).astype(BF16)

    def s(k):
        q = lax.div(slab, 2)
        lane = lax.broadcasted_iota(jnp.int32, (width, width), 1)
        part = jnp.dot(wt[k], s_v[...], preferred_element_type=F32)
        even = part[:, :width] + part[:, width : 2 * width]
        odd = part[:, 2 * width : 3 * width] + part[:, 3 * width :]
        even = pltpu.roll(even, lax.rem(width - q * rows_q, width), 1)
        odd = pltpu.roll(odd, lax.rem(width + rows_q - q * rows_q, width), 1)
        mine = jnp.where(lane < rows_q, even, jnp.where(lane < 2 * rows_q, odd, 0.0))
        for o in range(8):
            sub_mine[o, k * rows_q : (k + 1) * rows_q, :] = mine[o * rows_q : (o + 1) * rows_q]

    def s1():
        for j in range(3):
            first(j)

    def s4():
        total = last()
        square = jnp.concatenate([total, jnp.zeros_like(total)], axis=0)
        sub_out[...] = square.T[: 2 * rows_q, : 4 * rows_q]

    steps["S0",], steps["S1",], steps["S2",], steps["S3",], steps["S4",] = s0, s1, second, third, s4
    for k in range(CHUNKS):
        steps["S", k] = functools.partial(s, k)

    picked = pick(0)
    choose(picked, True)
    assert sorted(ORDER, key=str) == sorted(steps, key=str)
    for name in ORDER:
        steps[name]()
    for k in range(CHUNKS):
        links.finish(("R", k), sum_in.at[k, pl.ds(0, 7)])
        links.finish(("G", k), full.at[k, pl.ds(0, 15 * own)])
        for g in range(PARTS):
            links.finish(("F", k, g), panel_in.at[k, g, pl.ds(0, 7)])
    links.finish("S", sub_in.at[pl.ds(0, 7)])
    for kp in range(CHUNKS // 2):
        two = pl.ds(2 * kp, 2)
        pltpu.make_async_remote_copy(
            core_in.at[two], core_in.at[two], core_send.at[kp], core_recv.at[kp, 0],
            device_id=other_core, device_id_type=MESH,
        ).wait_send()


def hand_over(*arrays):
    def kernel(*refs):
        sources, targets, sem = refs[: len(arrays)], refs[len(arrays) : 2 * len(arrays)], refs[-1]
        copies = [
            pltpu.make_async_copy(source, target, sem.at[n])
            for n, (source, target) in enumerate(zip(sources, targets))
        ]
        for copy in copies:
            copy.start()
        for copy in copies:
            copy.wait()

    return pl.pallas_call(
        kernel,
        name="hand_over",
        out_shape=tuple(jax.ShapeDtypeStruct(v.shape, v.dtype) for v in arrays),
        in_specs=[pl.BlockSpec(memory_space=pltpu.VMEM)] * len(arrays),
        out_specs=tuple(pl.BlockSpec(memory_space=pl.ANY) for _ in arrays),
        scratch_shapes=[pltpu.SemaphoreType.DMA((len(arrays),))],
        compiler_params=pltpu.CompilerParams(vmem_limit_bytes=1 << 20),
    )(*arrays)


def body(pair_density, subspace, band_valence, band_conduction, occupied, energies):
    pairs, depth = pair_density.shape
    nb = subspace.shape[1]
    width, own, rows_q, cols = nb // CHUNKS, pairs // 16, nb // CHUNKS // 8, depth // PARTS
    vmem, dma = pltpu.VMEM, pltpu.SemaphoreType.DMA
    chi_panel, subspace_chi = pl.pallas_call(
        kernel,
        name="project",
        out_shape=(
            pltpu.VMEM((nb // 8, depth), F32),
            pltpu.VMEM((nb // 16, nb // 8), F32),
        ),
        in_specs=[
            pl.BlockSpec(memory_space=pl.ANY),
            pl.BlockSpec(memory_space=pl.ANY),
        ]
        + [pl.BlockSpec(memory_space=vmem)] * 4,
        out_specs=(pl.BlockSpec(memory_space=vmem), pl.BlockSpec(memory_space=vmem)),
        scratch_shapes=[
            vmem((1, pairs), F32),
            vmem((pairs, depth), BF16),
            vmem((depth, nb), BF16),
            vmem((depth, 2 * width), BF16),
            vmem((CHUNKS, pairs, width), F32),
            vmem((CHUNKS, pairs // 2, width), F32),
            vmem((CHUNKS, 8, own, width), F32),
            vmem((CHUNKS, pairs, width), F32),
            vmem((CHUNKS, width, pairs), BF16),
            vmem((CHUNKS, PARTS, width, cols), F32),
            vmem((CHUNKS, PARTS, 8, rows_q, cols), F32),
            vmem((8, nb // 8, width), F32),
            vmem((8, nb // 8, width), F32),
            dma((12,)),
            dma((CHUNKS // 2,)),
            dma((CHUNKS // 2, 4)),
            dma((CHUNKS * (2 + PARTS) + 1,)),
            dma((CHUNKS * (4 + 5) + CHUNKS * PARTS * 4 + 3,)),
        ],
        compiler_params=pltpu.CompilerParams(
            collective_id=0, has_side_effects=True, vmem_limit_bytes=62500000
        ),
    )(pair_density, subspace, band_valence[None, :], band_conduction[None, :], occupied[None, :], energies[None, :])
    return hand_over(chi_panel, subspace_chi)


def solution(mesh):
    return jax.shard_map(
        body,
        mesh=mesh,
        in_specs=(P("pair", "slab"), P("slab", None), P("pair"), P("pair"), P(), P()),
        out_specs=(P("pair", "slab"), P("slab", "pair")),
        check_vma=False,
    )
```

```python
import functools
import math

import jax
import jax.numpy as jnp
from jax import lax
from jax.experimental import pallas as pl
from jax.experimental.pallas import tpu as pltpu
from jax.sharding import PartitionSpec as P

MESH = pl.DeviceIdType.MESH
F32, BF16 = jnp.float32, jnp.bfloat16

CHUNKS = 4
TILE = 512
PARTS = 3
SUM_MODE = "BABB"
SPREAD_MODE = "BBAB"
PANEL_MODE = "BBABBBBBBBBB"
ORDER = (
    ("A", 0), ("A", 1), ("Q", 0, 0), ("Q", 1, 0), ("A", 2), ("L", 1), ("Q", 0, 1), ("Q", 0, 2),
    ("A", 3), ("Q", 0, 3), ("R2", 0), ("Q", 1, 1), ("Q", 1, 2), ("C",), ("B", 0), ("R3", 0),
    ("Q", 1, 3), ("R5", 0), ("R2", 1), ("L", 0), ("Q", 2, 0), ("B", 1), ("B", 2), ("R4", 0),
    ("B", 3), ("Q", 2, 1), ("Q", 2, 2), ("R3", 1), ("Q", 2, 3), ("Q", 3, 0), ("R2", 2), ("L", 2),
    ("L", 3), ("G2", 0), ("R4", 1), ("G5", 0), ("G3", 0), ("G2", 1), ("R5", 2), ("G5", 1),
    ("Q", 3, 1), ("R3", 2), ("G4", 0), ("V", 0), ("W", 0), ("G3", 1), ("F0", 0, 2, 0), ("F1", 0, 2),
    ("Q", 3, 2), ("Q", 3, 3), ("R2", 3), ("F0", 0, 1, 0), ("F1", 0, 1), ("F0", 0, 0, 0), ("R4", 2), ("F1", 0, 0),
    ("G4", 1), ("F2", 0, 2), ("V", 1), ("W", 1), ("R3", 3), ("F0", 1, 1, 0), ("R5", 3), ("F2", 0, 1),
    ("F0", 1, 2, 0), ("F1", 1, 1), ("F0", 1, 0, 0), ("G5", 2), ("F1", 1, 2), ("F1", 1, 0), ("F2", 0, 0), ("R4", 3),
    ("F2", 1, 1), ("F3", 0, 1), ("G2", 2), ("G3", 2), ("F5", 0, 1), ("F2", 1, 2), ("F2", 1, 0), ("F5", 0, 0),
    ("G2", 3), ("F5", 1, 1), ("F3", 1, 0), ("G5", 3), ("G4", 2), ("F3", 1, 1), ("V", 2), ("F5", 1, 2),
    ("W", 2), ("F5", 1, 0), ("G3", 3), ("F0", 2, 1, 0), ("F0", 2, 0, 0), ("F1", 2, 0), ("F1", 2, 1), ("F0", 2, 2, 0),
    ("F1", 2, 2), ("G4", 3), ("F3", 1, 2), ("V", 3), ("W", 3), ("F0", 3, 0, 0), ("F2", 2, 0), ("F1", 3, 0),
    ("F0", 3, 2, 0), ("F1", 3, 2), ("F0", 3, 1, 0), ("F1", 3, 1), ("F3", 2, 0), ("S0",), ("F4", 1, 0), ("F5", 2, 0),
    ("F2", 3, 0), ("F3", 3, 0), ("F2", 2, 2), ("F2", 2, 1), ("F2", 3, 2), ("S", 0), ("S", 1), ("F3", 2, 2),
    ("F2", 3, 1), ("S", 2), ("F3", 0, 0), ("F3", 2, 1), ("F3", 3, 1), ("S", 3), ("S1",), ("F5", 2, 1),
    ("F5", 2, 2), ("S2",), ("F5", 3, 0), ("F5", 3, 1), ("F3", 0, 2), ("F4", 0, 0), ("F3", 3, 2), ("F5", 3, 2),
    ("S3",), ("F4", 2, 2), ("F4", 1, 2), ("F4", 2, 1), ("F4", 2, 0), ("F4", 3, 0), ("F4", 0, 1), ("F4", 1, 1),
    ("F4", 3, 1), ("S4",), ("F4", 0, 2), ("F4", 3, 2),
)


class Links:
    def __init__(self, send_sem, recv_sem, device):
        self.send_sem, self.recv_sem, self.device = send_sem, recv_sem, device
        self.sent, self.received, self.size = {}, {}, {}

    def send(self, send_group, group, source, target, device):
        out = self.sent.setdefault(send_group, len(self.sent))
        back = self.received.setdefault(group, len(self.received))
        pltpu.make_async_remote_copy(
            source, target, self.send_sem.at[out], self.recv_sem.at[back], device_id=device, device_id_type=MESH
        ).start()
        amount = math.prod(source.shape)
        self.size["s", send_group] = self.size.get(("s", send_group), 0) + amount
        self.size["r", group] = self.size.get(("r", group), 0) + amount

    def _all(self, kind, group, at, ref):
        assert math.prod(ref.shape) == self.size[kind, group], group
        return pltpu.make_async_remote_copy(
            ref, ref, self.send_sem.at[at if kind == "s" else 0], self.recv_sem.at[at if kind == "r" else 0],
            device_id=self.device, device_id_type=MESH,
        )

    def wait(self, group, ref):
        self._all("r", group, self.received[group], ref).wait_recv()

    def finish(self, group, ref):
        self._all("s", group, self.sent[group], ref).wait_send()


def ring_sum(links, tag, mode, piece, slots, ring_up, ring_down, across, half):
    lo, hi = pl.ds(0, half), pl.ds(half, half)

    def add(ref, *others):
        total = ref[...]
        for other in others:
            total = total + other[...]
        ref[...] = total

    def send(group, source, slot, device):
        links.send(tag, (tag, group), source, slot, device)

    def wait(group, ref):
        links.wait((tag, group), ref)

    def first(j):
        if mode == "B":
            if j == 0:
                send("a", piece(2, 1), slots.at[6], across)
            if j == 1:
                send("b", piece(1, 1), slots.at[0], ring_up)
            if j == 2:
                send("b", piece(3, 1), slots.at[1], ring_down)
        else:
            if j == 0:
                send("a", piece(2, 0), slots.at[2], ring_up)
                send("a", piece(2, 1), slots.at[3], ring_down)
            if j == 1:
                send("b", piece(1, 1), slots.at[0], ring_up)
            if j == 2:
                send("d", piece(3, 0), slots.at[1], ring_down)

    def second():
        if mode == "B":
            wait("a", slots.at[6])
            add(piece(2, 0), slots.at[6])
            send("c", piece(2, 0).at[lo], slots.at[2, lo], ring_up)
            send("c", piece(2, 0).at[hi], slots.at[3, hi], ring_down)
        else:
            wait("a", slots.at[pl.ds(2, 2)])
            add(piece(1, 0), slots.at[2])
            send("d", piece(1, 0), slots.at[4], ring_up)
            add(piece(3, 1), slots.at[3])
            send("b", piece(3, 1), slots.at[5], ring_down)

    def third():
        wait("b", slots.at[pl.ds(0, 2)])
        add(piece(0, 1), slots.at[0], slots.at[1 if mode == "B" else 5])
        send("d", piece(0, 1), slots.at[7], across)

    def fourth():
        wait("c", slots.at[2])
        add(piece(1, 0).at[lo], slots.at[2, lo])
        send("d", piece(1, 0), slots.at[4], ring_up)
        add(piece(3, 0).at[hi], slots.at[3, hi])
        send("d", piece(3, 0), slots.at[5], ring_down)

    def last():
        wait("d", slots.at[pl.ds(4, 3)])
        return piece(0, 0)[...] + slots[5 if mode == "B" else 1] + slots[4] + slots[7]

    return first, second, third, fourth, last


def kernel(
    a_hbm, s_hbm, valence_ref, conduction_ref, occupied_ref, energies_ref, chi_out, sub_out,
    w_ref, a_v, s_v, sp, coeff, core_in, sum_in, full, wt, chi, panel_in, sub_mine, sub_in,
    load_sem, core_send, core_recv, send_sem, recv_sem,
):
    pairs, depth = a_v.shape
    nb = s_v.shape[1]
    width = nb // CHUNKS
    block = pairs // 8
    own = block // 2
    rows_q = width // 8
    cols = depth // PARTS

    pair, slab = lax.axis_index("pair"), lax.axis_index("slab")
    y_hi, x = lax.div(pair, 4), lax.rem(pair, 4)
    y_lo, z, core = lax.div(slab, 8), lax.rem(lax.div(slab, 2), 4), lax.rem(slab, 2)

    def slab_of(y, zz, c):
        return (pair, y * 8 + zz * 2 + c)

    def pair_of(y, xx):
        return (y * 4 + xx, slab)

    def up(v, d):
        return lax.rem(v + d, 4)

    z_up, z_down = slab_of(y_lo, up(z, 1), core), slab_of(y_lo, up(z, 3), core)
    y_across, other_core = slab_of(1 - y_lo, z, core), slab_of(y_lo, z, 1 - core)
    x_up, x_down, hi_across = pair_of(y_hi, up(x, 1)), pair_of(y_hi, up(x, 3)), pair_of(1 - y_hi, x)

    Z_ORDER = (2, 1, 3, 0)

    def block_rows(core_at, j):
        return pl.ds(pl.multiple_of((core_at * 4 + up(z, Z_ORDER[j])) * block, block), block)

    def half_rows(j):
        return pl.ds(pl.multiple_of(up(z, Z_ORDER[j]) * block, block), block)

    def side(i):
        return jnp.where(i == 0, 1 - core, core)

    def a_load(j, i):
        rows = block_rows(side(i), j)
        return pltpu.make_async_copy(a_hbm.at[rows], a_v.at[rows], load_sem.at[2 * j + i])

    barrier = pltpu.get_barrier_semaphore()
    greeted = [other_core, z_up, z_down, y_across, x_up, x_down, hi_across]
    for device in greeted:
        pl.semaphore_signal(barrier, inc=1, device_id=device, device_id_type=MESH)

    def s_load(i):
        rows = pl.ds(pl.multiple_of(i * 2 * block, 2 * block), 2 * block)
        return pltpu.make_async_copy(s_hbm.at[rows], s_v.at[rows], load_sem.at[8 + i])

    for i in range(4):
        s_load(i).start()
    for j in range(4):
        for i in range(2):
            a_load(j, i).start()

    links = Links(send_sem, recv_sem, other_core)

    def pick(kp):
        to = lax.broadcasted_iota(jnp.int32, (1, 2 * width), 1)
        frm = lax.broadcasted_iota(jnp.int32, (nb, 2 * width), 0)
        k = kp * 2 + to // width
        b = (lax.rem(to, width) // rows_q) * (nb // 8) + k * rows_q + lax.rem(to, rows_q)
        return jnp.where(frm == b, 1.0, 0.0).astype(BF16)

    def choose(picked, loading):
        @pl.loop(0, 4)
        def _(i):
            if loading:
                s_load(i).wait()
            rows = pl.ds(pl.multiple_of(i * 2 * block, 2 * block), 2 * block)
            sp[rows, :] = jnp.dot(s_v[rows, :], picked, preferred_element_type=F32).astype(BF16)

    def core_copy(kp, j):
        two = pl.ds(2 * kp, 2)
        return pltpu.make_async_remote_copy(
            coeff.at[two, block_rows(1 - core, j)], core_in.at[two, half_rows(j)], core_send.at[kp], core_recv.at[kp, j],
            device_id=other_core, device_id_type=MESH,
        )

    def part_of_product(kp, j, i):
        rows = block_rows(side(i), j)
        if kp == 0:
            a_load(j, i).wait()
        part = jnp.dot(a_v[rows, :], sp[...], preferred_element_type=F32)
        for h in range(2):
            coeff[2 * kp + h, rows, :] = part[:, h * width : (h + 1) * width]

    def to_other_core(kp, j):
        core_copy(kp, j).start()

    def product(kp, j):
        @pl.loop(0, 2)
        def _(i):
            part_of_product(kp, j, i)

            @pl.when(i == 0)
            def _():
                if kp == 0 and j == 0:
                    pl.semaphore_wait(barrier, len(greeted))
                to_other_core(kp, j)

    def weights(j):
        at = slice(j * (pairs // 4), (j + 1) * (pairs // 4))
        bands = energies_ref.shape[1]
        energy = energies_ref[...]
        high = energy.astype(BF16).astype(F32)
        middle = (energy - high).astype(BF16).astype(F32)
        low = energy - high - middle
        row = lax.broadcasted_iota(jnp.int32, (16, bands), 0)
        table = jnp.where(row == 0, high, jnp.where(row == 1, middle, jnp.where(row == 2, low, 0.0)))
        table = jnp.where(row == 3, occupied_ref[...].astype(F32), table).astype(BF16)
        band = lax.broadcasted_iota(jnp.int32, (bands, pairs // 4), 0)

        def lookup(indices):
            one_hot = jnp.where(band == indices, 1.0, 0.0).astype(BF16)
            found = jnp.dot(table, one_hot, preferred_element_type=F32)
            return found[0:1] + found[1:2] + found[2:3], found[3:4]

        energy_low, filled_low = lookup(valence_ref[:, at])
        energy_high, filled_high = lookup(conduction_ref[:, at])
        scale = 1.0 / math.sqrt(pairs * 8)
        w_ref[:, at] = -2.0 * filled_low * (1.0 - filled_high) / (jnp.abs(energy_high - energy_low) + 0.5) * scale

    def owner_rows(z_at, y_at):
        return pl.ds(pl.multiple_of((core * 4 + z_at) * block + y_at * own, own), own)

    steps = {}
    for k in range(CHUNKS):
        get = lambda dr, da, k=k: coeff.at[k, owner_rows(up(z, dr), (1 - y_lo) if da else y_lo)]
        first, second, third, fourth, last = ring_sum(
            links, ("R", k), SUM_MODE[k], get, sum_in.at[k], z_up, z_down, y_across, own // 2
        )

        def gather(j, k=k, first=first):
            if k % 2 == 0:
                core_copy(k // 2, j).wait_recv()
            here = block_rows(core, j)
            coeff[k, here, :] = coeff[k, here, :] + core_in[k, half_rows(j), :]
            first(j)

        for j in range(4):
            steps["Q", k, j] = functools.partial(gather, j)

        def spread(group, z_at, y_at, device, k=k, part=None):
            rows = owner_rows(z_at, y_at)
            if part is not None:
                start = (core * 4 + z_at) * block + y_at * own + part * (own // 2)
                rows = pl.ds(pl.multiple_of(start, own // 2), own // 2)
            links.send(("G", k), (group, k), full.at[k, rows], full.at[k, rows], device)

        def arrived(group, pieces, k=k):
            links.wait((group, k), full.at[k, pl.ds(0, pieces * own)])

        whole = SPREAD_MODE[k] == "A"

        def r4(k=k, last=last, spread=spread):
            full[k, owner_rows(z, y_lo), :] = last()
            spread("y", z, y_lo, y_across)
            spread("p", z, y_lo, z_up)
            spread("p", z, y_lo, z_down)
            spread("core", z, y_lo, other_core)

        def g2(spread=spread, arrived=arrived, whole=whole):
            arrived("p", 2)
            if whole:
                spread("l", up(z, 3), y_lo, z_up)
            else:
                spread("h", up(z, 3), y_lo, z_up, part=0)
                spread("h", up(z, 1), y_lo, z_down, part=1)
            spread("core", up(z, 3), y_lo, other_core)
            spread("core", up(z, 1), y_lo, other_core)

        def g5(spread=spread, arrived=arrived, whole=whole):
            arrived("y", 1)
            spread("l", z, 1 - y_lo, z_up)
            spread("h" if whole else "l", z, 1 - y_lo, z_down)
            spread("core", z, 1 - y_lo, other_core)

        def g3(spread=spread, arrived=arrived, whole=whole):
            arrived("h", 1)
            if whole:
                spread("l", up(z, 1), 1 - y_lo, z_down)
                spread("core", up(z, 1), 1 - y_lo, other_core)
            else:
                spread("l", up(z, 2), y_lo, y_across)
                spread("core", up(z, 2), y_lo, other_core)

        def weigh(core_at, k=k):
            for i in range(4):
                at = pl.ds(pl.multiple_of((core_at * 4 + i) * block, block), block)
                wt[k, :, at] = (full[k, at, :].T * w_ref[:, at]).astype(BF16)

        def g4(spread=spread, arrived=arrived, whole=whole):
            arrived("l", 3)
            spread("core", up(z, 3), 1 - y_lo, other_core)
            if whole:
                spread("core", up(z, 2), y_lo, other_core)
            else:
                spread("core", up(z, 1), 1 - y_lo, other_core)
            spread("core", up(z, 2), 1 - y_lo, other_core)

        def w1(arrived=arrived, weigh=weigh):
            arrived("core", 8)
            weigh(1 - core)

        steps["R2", k], steps["R3", k], steps["R4", k], steps["W", k] = second, third, r4, w1
        steps["G2", k], steps["G5", k], steps["G3", k], steps["G4", k] = g2, g5, g3, g4
        steps["V", k] = functools.partial(weigh, core)
        if SUM_MODE[k] == "B":
            steps["R5", k] = fourth

        for g in range(PARTS):
            def rows_of(dx, dy, k=k, g=g):
                q = ((1 - y_hi) if dy else y_hi) * 4 + up(x, dx)
                return chi.at[k, g, pl.ds(pl.multiple_of(q * rows_q, rows_q), rows_q)]

            first, second, third, fourth, last = ring_sum(
                links, ("F", k, g), PANEL_MODE[k * PARTS + g], rows_of, panel_in.at[k, g], x_up, x_down, hi_across, rows_q // 2
            )

            def tile(i, k=k, g=g):
                src, dst = pl.ds(g * cols + i * TILE, TILE), pl.ds(i * TILE, TILE)
                chi[k, g, :, dst] = jnp.dot(wt[k], a_v[:, src], preferred_element_type=F32)

            def f1(tile=tile, first=first):
                tile(cols // TILE - 1)
                for j in range(3):
                    first(j)

            for i in range(cols // TILE - 1):
                steps["F0", k, g, i] = functools.partial(tile, i)

            def f4(k=k, g=g, last=last):
                chi_out[k * rows_q : (k + 1) * rows_q, g * cols : (g + 1) * cols] = last()

            steps["F1", k, g], steps["F2", k, g], steps["F3", k, g], steps["F4", k, g] = f1, second, third, f4
            if PANEL_MODE[k * PARTS + g] == "B":
                steps["F5", k, g] = fourth

    for j in range(4):
        steps["A", j] = functools.partial(product, 0, j)
        steps["L", j] = functools.partial(weights, j)
        steps["B", j] = functools.partial(product, 1, j)
    steps["C",] = lambda: choose(pick(1), False)

    first, second, third, _, last = ring_sum(
        links, "S", "A",
        lambda dx, dy: sub_mine.at[((1 - y_hi) if dy else y_hi) * 4 + up(x, dx)],
        sub_in, x_up, x_down, hi_across, 0,
    )

    def s0():
        for i in range(8):
            at = pl.ds(i * block, block)
            for h in range(2):
                value = full[2 * core + h, at, :]
                high = value.astype(BF16)
                s_v[at, 2 * h * width : (2 * h + 1) * width] = high
                s_v[at, (2 * h + 1) * width : (2 * h + 2) * width] = (value - high.astype(F32)).astype(BF16)

    def s(k):
        q = lax.div(slab, 2)
        lane = lax.broadcasted_iota(jnp.int32, (width, width), 1)
        part = jnp.dot(wt[k], s_v[...], preferred_element_type=F32)
        even = part[:, :width] + part[:, width : 2 * width]
        odd = part[:, 2 * width : 3 * width] + part[:, 3 * width :]
        even = pltpu.roll(even, lax.rem(width - q * rows_q, width), 1)
        odd = pltpu.roll(odd, lax.rem(width + rows_q - q * rows_q, width), 1)
        mine = jnp.where(lane < rows_q, even, jnp.where(lane < 2 * rows_q, odd, 0.0))
        for o in range(8):
            sub_mine[o, k * rows_q : (k + 1) * rows_q, :] = mine[o * rows_q : (o + 1) * rows_q]

    def s1():
        for j in range(3):
            first(j)

    def s4():
        total = last()
        square = jnp.concatenate([total, jnp.zeros_like(total)], axis=0)
        sub_out[...] = square.T[: 2 * rows_q, : 4 * rows_q]

    steps["S0",], steps["S1",], steps["S2",], steps["S3",], steps["S4",] = s0, s1, second, third, s4
    for k in range(CHUNKS):
        steps["S", k] = functools.partial(s, k)

    picked = pick(0)
    choose(picked, True)
    assert sorted(ORDER, key=str) == sorted(steps, key=str)
    for name in ORDER:
        steps[name]()
    for k in range(CHUNKS):
        links.finish(("R", k), sum_in.at[k, pl.ds(0, 7)])
        links.finish(("G", k), full.at[k, pl.ds(0, 15 * own)])
        for g in range(PARTS):
            links.finish(("F", k, g), panel_in.at[k, g, pl.ds(0, 7)])
    links.finish("S", sub_in.at[pl.ds(0, 7)])
    for kp in range(CHUNKS // 2):
        two = pl.ds(2 * kp, 2)
        pltpu.make_async_remote_copy(
            core_in.at[two], core_in.at[two], core_send.at[kp], core_recv.at[kp, 0],
            device_id=other_core, device_id_type=MESH,
        ).wait_send()


def hand_over(*arrays):
    def kernel(*refs):
        sources, targets, sem = refs[: len(arrays)], refs[len(arrays) : 2 * len(arrays)], refs[-1]
        copies = []
        for n, (source, target) in enumerate(zip(sources, targets)):
            rows = source.shape[0] // 4
            for i in range(4):
                at = pl.ds(i * rows, rows)
                copies.append(pltpu.make_async_copy(source.at[at], target.at[at], sem.at[n, i]))
        for copy in copies:
            copy.start()
        for copy in copies:
            copy.wait()

    return pl.pallas_call(
        kernel,
        name="hand_over",
        out_shape=tuple(jax.ShapeDtypeStruct(v.shape, v.dtype) for v in arrays),
        in_specs=[pl.BlockSpec(memory_space=pltpu.VMEM)] * len(arrays),
        out_specs=tuple(pl.BlockSpec(memory_space=pl.ANY) for _ in arrays),
        scratch_shapes=[pltpu.SemaphoreType.DMA((len(arrays), 4))],
        compiler_params=pltpu.CompilerParams(vmem_limit_bytes=1 << 20),
    )(*arrays)


def body(pair_density, subspace, band_valence, band_conduction, occupied, energies):
    pairs, depth = pair_density.shape
    nb = subspace.shape[1]
    width, own, rows_q, cols = nb // CHUNKS, pairs // 16, nb // CHUNKS // 8, depth // PARTS
    vmem, dma = pltpu.VMEM, pltpu.SemaphoreType.DMA
    chi_panel, subspace_chi = pl.pallas_call(
        kernel,
        name="project",
        out_shape=(
            pltpu.VMEM((nb // 8, depth), F32),
            pltpu.VMEM((nb // 16, nb // 8), F32),
        ),
        in_specs=[
            pl.BlockSpec(memory_space=pl.ANY),
            pl.BlockSpec(memory_space=pl.ANY),
        ]
        + [pl.BlockSpec(memory_space=vmem)] * 4,
        out_specs=(pl.BlockSpec(memory_space=vmem), pl.BlockSpec(memory_space=vmem)),
        scratch_shapes=[
            vmem((1, pairs), F32),
            vmem((pairs, depth), BF16),
            vmem((depth, nb), BF16),
            vmem((depth, 2 * width), BF16),
            vmem((CHUNKS, pairs, width), F32),
            vmem((CHUNKS, pairs // 2, width), F32),
            vmem((CHUNKS, 8, own, width), F32),
            vmem((CHUNKS, pairs, width), F32),
            vmem((CHUNKS, width, pairs), BF16),
            vmem((CHUNKS, PARTS, width, cols), F32),
            vmem((CHUNKS, PARTS, 8, rows_q, cols), F32),
            vmem((8, nb // 8, width), F32),
            vmem((8, nb // 8, width), F32),
            dma((12,)),
            dma((CHUNKS // 2,)),
            dma((CHUNKS // 2, 4)),
            dma((CHUNKS * (2 + PARTS) + 1,)),
            dma((CHUNKS * (4 + 5) + CHUNKS * PARTS * 4 + 3,)),
        ],
        compiler_params=pltpu.CompilerParams(
            collective_id=0, has_side_effects=True, vmem_limit_bytes=62500000
        ),
    )(pair_density, subspace, band_valence[None, :], band_conduction[None, :], occupied[None, :], energies[None, :])
    return hand_over(chi_panel, subspace_chi)


def solution(mesh):
    return jax.shard_map(
        body,
        mesh=mesh,
        in_specs=(P("pair", "slab"), P("slab", None), P("pair"), P("pair"), P(), P()),
        out_specs=(P("pair", "slab"), P("slab", "pair")),
        check_vma=False,
    )
```
